128 devices in a mesh: ep: 4 (over z), tm: 32 (over y, x, core).
Axes of the slice: x: 4, y: 4, z: 4, core: 2. Of those that a mesh axis runs over, the one named last changes fastest.
Arguments:
- states: bfloat16 [24, 4096, 1024], P('ep', 'tm'), may hold values from -26 to 26
- norm_gain: float32 [1024], replicated, may hold values from 0.25 to 4
- w_query: bfloat16 [1024, 1024], replicated, may hold values from -0.1875 to 0.1875
- w_keyval: bfloat16 [1024, 2048], replicated, may hold values from -0.1875 to 0.1875
- w_out: bfloat16 [1024, 1024], replicated, may hold values from -0.1875 to 0.1875
- rel_bias: float32 [8, 256], replicated, may hold values from -2.5 to 160
- w_policy: bfloat16 [1024, 128], replicated, may hold values from -8.125 to 8.125
- w_value: bfloat16 [1024], replicated, may hold values from -0.1875 to 0.1875
- actions: int32 [24, 4096], P('ep', 'tm'), may hold values from 0 to 127
- legal_mask: int32 [24, 4096, 128], P('ep', 'tm'), may hold values from 0 to 1, as said below
- rewards: int32 [24, 4096], P('ep', 'tm'), may hold values from -1 to 1
- episode_end: int32 [24, 4096], P('ep', 'tm'), may hold values from 0 to 1
- behavior_logprob: float32 [24, 4096], P('ep', 'tm'), may hold values from -8 to 0
- reg_logprob: float32 [24, 4096], P('ep', 'tm'), may hold values from -8 to 0
Outputs:
- grads: float32 [1024, 4224], P(('ep', 'tm'))
The draws below stay inside these ranges and needn't reach their ends.
Inputs may be any that keep to these rules, and one draw needn't show every extreme that they name: legal_mask is 1 at the sampled action of every step.
All inputs are finite; a program needn't handle non-finite values.
Results may differ from the reference program's by a relative error of at most 0.012.
Values may be sent and summed in bfloat16 or wider, within the bound.
No kernel may reach another device: no remote copies, remote signals or barrier semaphores. Data moves between devices by JAX's collectives and lax.ppermute only.
A program may use at most 128 MiB of HBM per device.

```python
import math
import jax
import jax.numpy as jnp
from jax import lax

D = 1024
HEADS = 8
ACTIONS = 128
SEG = 128
EPIS = 24
ROLLOUT_MOVES = 4096


def feature_ramp(key, lowest, highest):
    places = lax.broadcasted_iota(jnp.float32, (D,), 0) / max(D - 1, 1)
    rough = jnp.exp(jax.random.uniform(key, (D,), jnp.float32, -0.35, 0.35))
    return jnp.exp(math.log(lowest) + places * (math.log(highest) - math.log(lowest))) * rough


def draw_states(key, part):
    first_key, seed_number_two = jax.random.split(jax.random.fold_in(key, 61))
    base = jnp.clip(jax.random.normal(first_key, (EPIS, ROLLOUT_MOVES, D), jnp.float32), -6.0, 6.0)
    scales = feature_ramp(seed_number_two, 0.5, 2.0)
    return (base * scales[None, None, :]).astype(jnp.bfloat16)


def draw_norm_gain(key, part):
    ramp_key = jax.random.fold_in(key, 67)
    scales = feature_ramp(ramp_key, 0.5, 1.5)
    return scales.astype(jnp.float32)


def joint_moves(key):
    base_key = jax.random.fold_in(key, 7)
    first_key, seed_number_two = jax.random.split(base_key)
    sampled = jax.random.randint(first_key, (EPIS, ROLLOUT_MOVES), 0, ACTIONS)
    coins = jax.random.randint(seed_number_two, (EPIS, ROLLOUT_MOVES, ACTIONS), 0, 2)
    onehot = (lax.broadcasted_iota(jnp.int32, (EPIS, ROLLOUT_MOVES, ACTIONS), 2) == sampled[:, :, None]).astype(jnp.int32)
    return (sampled.astype(jnp.int32), jnp.maximum(coins, onehot).astype(jnp.int32))


def trajectory_rank(key):
    return jax.random.permutation(jax.random.fold_in(key, 31), EPIS).astype(jnp.int32)


def draw_actions(key, part):
    return joint_moves(key)[0]


def draw_legal_mask(key, part):
    return joint_moves(key)[1]


def draw_episode_end(key, part):
    ranking = trajectory_rank(key)
    coins = jax.random.randint(jax.random.fold_in(key, 37), (EPIS, ROLLOUT_MOVES), 0, SEG)
    ending = ranking >= EPIS - EPIS // 4
    return jnp.where(ending[:, None] & (coins == 0), 1, 0).astype(jnp.int32)


def draw_behavior_logprob(key, part):
    ranking = trajectory_rank(key)
    first_key, seed_number_two, seed_number_three, fourth_key, fifth_key = jax.random.split(jax.random.fold_in(key, 41), 5)
    midpoint_logscale = math.log(ACTIONS / 2.0)
    tensor_extent = (EPIS, ROLLOUT_MOVES)
    starting_estimate = -midpoint_logscale - jax.random.uniform(first_key, tensor_extent, jnp.float32, 2.0, 3.0)
    episode_offset = jax.random.randint(seed_number_two, tensor_extent, 0, ROLLOUT_MOVES) < 3
    episode_span = -midpoint_logscale + jax.random.uniform(seed_number_three, tensor_extent, jnp.float32, 0.1, 0.5)
    cut_at = jax.random.randint(fourth_key, tensor_extent, 0, SEG) < 3
    cut = -midpoint_logscale + jax.random.uniform(fifth_key, tensor_extent, jnp.float32, 1.5, 2.0)
    forgetful = ranking >= EPIS // 2
    overall_outcome = jnp.where(episode_offset, episode_span, starting_estimate)
    overall_outcome = jnp.where(forgetful[:, None] & cut_at, cut, overall_outcome)
    return overall_outcome.astype(jnp.float32)


def draw_reg_logprob(key, part):
    midpoint_logscale = math.log(ACTIONS / 2.0)
    tensor_extent = (EPIS, ROLLOUT_MOVES)
    offset = jax.random.uniform(jax.random.fold_in(key, 53), tensor_extent, jnp.float32, -1.0, 1.0)
    return (-midpoint_logscale - 0.12 + offset).astype(jnp.float32)


def draw_rel_bias(key, part):
    first_key = jax.random.fold_in(jax.random.fold_in(key, 11), 0)
    starting_estimate = jnp.clip(0.5 * jax.random.normal(first_key, (HEADS, 2 * SEG), jnp.float32), -2.5, 2.5)
    return starting_estimate.astype(jnp.float32)


def draw_w_policy(key, part):
    first_key = jax.random.fold_in(jax.random.fold_in(key, 23), 0)
    starting_estimate = jnp.clip(jax.random.normal(first_key, (D, ACTIONS), jnp.float32), -4.0, 4.0) * (0.3 / math.sqrt(D))
    return starting_estimate.astype(jnp.bfloat16)


def place_ends(entries, stream_key, low, top_value):
    longest = entries.shape.index(max(entries.shape))
    spots = []
    for shift in (0, 1):
        where = [jax.random.randint(jax.random.fold_in(stream_key, axis), (), 0, length) for axis, length in enumerate(entries.shape)]
        where[longest] = (where[longest] + shift) % entries.shape[longest]
        spots.append(tuple(where))
    return entries.at[spots[0]].set(low).at[spots[1]].set(top_value)


def noise(key, dims, scale, limit, kind=jnp.bfloat16):
    return jnp.clip(scale * jax.random.normal(key, dims, jnp.float32), -limit, limit).astype(kind)


def setup_inputs(seed: int = 0) -> dict:
    key_of = jax.random.split(jax.random.key(seed), 15)
    return {
        "states": draw_states(jax.random.fold_in(key_of[14], 71), 0),
        "norm_gain": draw_norm_gain(jax.random.fold_in(key_of[14], 71), 0),
        "w_query": noise(key_of[2], (D, D), D ** -0.5, 0.1875),
        "w_keyval": noise(key_of[3], (D, 2 * D), D ** -0.5, 0.1875),
        "w_out": noise(key_of[4], (D, D), D ** -0.5, 0.1875),
        "rel_bias": draw_rel_bias(jax.random.fold_in(key_of[14], 71), 0),
        "w_policy": draw_w_policy(jax.random.fold_in(key_of[14], 71), 0),
        "w_value": noise(key_of[7], (D,), D ** -0.5, 0.1875),
        "actions": draw_actions(jax.random.fold_in(key_of[14], 71), 0),
        "legal_mask": draw_legal_mask(jax.random.fold_in(key_of[14], 71), 0),
        "rewards": place_ends(jax.random.randint(key_of[10], (EPIS, ROLLOUT_MOVES), -1, 2), jax.random.fold_in(key_of[10], 1), -1, 1).astype(jnp.int32),
        "episode_end": draw_episode_end(jax.random.fold_in(key_of[14], 71), 0),
        "behavior_logprob": draw_behavior_logprob(jax.random.fold_in(key_of[14], 71), 0),
        "reg_logprob": draw_reg_logprob(jax.random.fold_in(key_of[14], 71), 0),
    }


norm_eps = 1e-06
grad_eps = 1e-06
reg_weight = 0.2
adv_clip = 20.0
masked_score = -1e+30

def rms_norm(states, norm_gain):
    widened = states.astype(jnp.float32)
    spread = lax.optimization_barrier(jnp.mean(widened * widened, axis=-1, keepdims=True))
    return (widened * lax.rsqrt(spread + norm_eps) * norm_gain).astype(jnp.bfloat16)

def make_allowed(has_memory, length):
    row_index = lax.broadcasted_iota(jnp.int32, (length, 2 * length), 0)
    col_index = lax.broadcasted_iota(jnp.int32, (length, 2 * length), 1)
    current = col_index - length <= row_index
    in_memory = col_index < length
    return jnp.where(in_memory[None], has_memory[:, None, None], current[None])

def attend(queries, key_rows, value_rows, bias_grid, allowed):
    batch_size, length, model_width = queries.shape
    head_count = bias_grid.shape[0]
    head_dim = model_width // head_count
    query_heads = queries.reshape(batch_size, length, head_count, head_dim).astype(jnp.float32)
    key_heads = key_rows.reshape(batch_size, 2 * length, head_count, head_dim).astype(jnp.float32)
    value_heads = value_rows.reshape(batch_size, 2 * length, head_count, head_dim).astype(jnp.float32)
    scores = jnp.einsum('bqhd,bkhd->bhqk', query_heads, key_heads) / math.sqrt(head_dim) + bias_grid[None]
    scores = jnp.where(allowed[:, None], scores, masked_score)
    highest = lax.stop_gradient(lax.optimization_barrier(jnp.max(scores, axis=-1, keepdims=True)))
    weights = jnp.exp(scores - highest)
    weights = weights / lax.optimization_barrier(jnp.sum(weights, axis=-1, keepdims=True))
    weights = lax.optimization_barrier(weights.astype(jnp.bfloat16)).astype(jnp.float32)
    mixed_heads = jnp.einsum('bhqk,bkhd->bqhd', weights, value_heads)
    return mixed_heads.reshape(batch_size, length, model_width).astype(jnp.bfloat16)

def taken_logprob(logits, legal_mask, actions):
    legal_flags = legal_mask > 0
    highest = lax.optimization_barrier(jnp.max(jnp.where(legal_flags, logits, masked_score), axis=-1, keepdims=True))
    partition = lax.optimization_barrier(jnp.sum(jnp.where(legal_flags, jnp.exp(logits - highest), 0.0), axis=-1, keepdims=True))
    chosen = lax.broadcasted_iota(jnp.int32, logits.shape, 1) == actions[:, None]
    picked = lax.optimization_barrier(jnp.sum(jnp.where(chosen, logits, 0.0), axis=-1, keepdims=True))
    return ((picked - highest - jnp.log(partition))[:, 0], chosen, legal_flags)

def bias_lookup(rel_bias):
    bias_span = rel_bias.shape[1]
    length = bias_span // 2
    row_index = jnp.arange(length)[:, None]
    col_index = jnp.arange(bias_span)[None, :]
    lookup = jnp.clip(row_index - col_index + length, 0, bias_span - 1).astype(jnp.int32)
    return jnp.take(rel_bias, lookup, axis=1)

def contract_rows(left_rows, right_rows):
    return lax.dot_general(left_rows, right_rows, (((0,), (0,)), ((), ())), preferred_element_type=jnp.float32)

def reference(states, norm_gain, w_query, w_keyval, w_out, rel_bias, w_policy, w_value, actions, legal_mask, rewards, episode_end, behavior_logprob, reg_logprob):
    episodes, time_len, model_width = states.shape
    length = SEG
    blocks = time_len // length
    batch_size = episodes * blocks
    normed = rms_norm(states, norm_gain).reshape(episodes, blocks, length, model_width)
    memory = jnp.concatenate([jnp.zeros_like(normed[:, :1]), normed[:, :-1]], axis=1)
    key_input = jnp.concatenate([memory, normed], axis=2).reshape(batch_size * 2 * length, model_width)
    flat_normed = normed.reshape(batch_size * length, model_width)
    queries = jnp.dot(flat_normed, w_query, preferred_element_type=jnp.float32).astype(jnp.bfloat16).reshape(batch_size, length, model_width)
    keyvals = jnp.dot(key_input, w_keyval, preferred_element_type=jnp.float32).astype(jnp.bfloat16).reshape(batch_size, 2 * length, 2 * model_width)
    bias_grid = bias_lookup(rel_bias)
    has_memory = jnp.arange(batch_size) % blocks > 0
    allowed = make_allowed(has_memory, length)

    def attention_core(query_part, key_part, value_part):
        return attend(query_part, key_part, value_part, bias_grid, allowed)
    attended, pullback = jax.vjp(attention_core, queries, keyvals[:, :, :model_width], keyvals[:, :, model_width:])
    flat_att = attended.reshape(batch_size * length, model_width)
    projected = jnp.dot(flat_att, w_out, preferred_element_type=jnp.float32)
    hidden = (states.reshape(-1, model_width).astype(jnp.float32) + projected).astype(jnp.bfloat16)
    logits = jnp.dot(hidden, w_policy, preferred_element_type=jnp.float32)
    values = jnp.dot(hidden, w_value, preferred_element_type=jnp.float32).reshape(episodes, time_len)
    log_flat, chosen, legal_flags = taken_logprob(logits, legal_mask.reshape(-1, logits.shape[1]), actions.reshape(-1))
    log_taken = log_flat.reshape(episodes, time_len)
    clipped = jnp.minimum(1.0, jnp.exp(log_taken - behavior_logprob))
    shaped = rewards.astype(jnp.float32) - reg_weight * (log_taken - reg_logprob)
    carry_on = 1.0 - episode_end.astype(jnp.float32)
    next_values = jnp.concatenate([values[:, 1:], jnp.zeros((episodes, 1), jnp.float32)], axis=1)
    td_error = clipped * (shaped + carry_on * next_values - values)
    trace_decay = carry_on * clipped

    def step_back(running, inputs):
        running = inputs[0] + inputs[1] * running
        return (running, running)
    unused_end, target_gap = lax.scan(step_back, jnp.zeros((episodes,), jnp.float32), (td_error.T, trace_decay.T), reverse=True)
    targets = values + target_gap.T
    next_targets = jnp.concatenate([targets[:, 1:], jnp.zeros((episodes, 1), jnp.float32)], axis=1)
    spread = (shaped + carry_on * next_targets - values) * jnp.exp(-behavior_logprob)
    taken_prob = jnp.exp(log_taken)
    adv_taken = jnp.clip((1.0 - taken_prob) * spread, -adv_clip, adv_clip).reshape(-1, 1)
    adv_other = jnp.clip(-taken_prob * spread, -adv_clip, adv_clip).reshape(-1, 1)
    logit_cot = jnp.where(legal_flags, -jnp.where(chosen, adv_taken, adv_other), 0.0).astype(jnp.bfloat16)
    value_cot = (values - targets).reshape(-1, 1)
    hidden_cot = lax.dot_general(logit_cot, w_policy, (((1,), (1,)), ((), ())), preferred_element_type=jnp.float32)
    hidden_cot = (hidden_cot + value_cot * w_value.astype(jnp.float32)[None, :]).astype(jnp.bfloat16)
    att_cot = lax.dot_general(hidden_cot, w_out, (((1,), (1,)), ((), ())), preferred_element_type=jnp.float32)
    att_cot = att_cot.astype(jnp.bfloat16).reshape(batch_size, length, model_width)
    grad_query, grad_keys, grad_values = pullback(att_cot)
    grad_kv = jnp.concatenate([grad_keys, grad_values], axis=2).reshape(-1, 2 * model_width)
    raw_grads = jnp.concatenate([contract_rows(flat_normed, grad_query.reshape(-1, model_width)), contract_rows(key_input, grad_kv), contract_rows(flat_att, hidden_cot), contract_rows(hidden, logit_cot)], axis=1)
    grand_total = jnp.sum(raw_grads * raw_grads)
    clip_scale = jnp.minimum(1.0, math.sqrt(raw_grads.size) / jnp.sqrt(grand_total + grad_eps))
    return raw_grads * clip_scale
```

```python
import math

import jax
import jax.numpy as jnp
from jax import lax
from jax.sharding import Mesh
from jax.sharding import PartitionSpec as P

norm_eps = 1e-06
grad_eps = 1e-06
reg_weight = 0.2
adv_clip = 20.0
masked_score = -1e30
EVERY = ("z", "y", "x", "c")
TIME = ("y", "x", "c")


def passed_along(value, axis, steps):
    count = lax.axis_size(axis)
    first, last = (max(0, -steps), min(count, count - steps))
    return lax.ppermute(value, axis, [(source, source + steps) for source in range(first, last)])


def rms_norm(states, norm_gain):
    widened = states.astype(jnp.float32)
    spread = jnp.mean(widened * widened, axis=-1, keepdims=True)
    return (widened * lax.rsqrt(spread + norm_eps) * norm_gain).astype(jnp.bfloat16)


def make_allowed(has_memory, length):
    row_index = lax.broadcasted_iota(jnp.int32, (length, 2 * length), 0)
    col_index = lax.broadcasted_iota(jnp.int32, (length, 2 * length), 1)
    current = col_index - length <= row_index
    in_memory = col_index < length
    return jnp.where(in_memory[None], has_memory[:, None, None], current[None])


def attend(queries, key_rows, value_rows, bias_grid, allowed):
    batch_size, length, model_width = queries.shape
    head_count = bias_grid.shape[0]
    head_dim = model_width // head_count
    query_heads = queries.reshape(batch_size, length, head_count, head_dim).astype(jnp.float32)
    key_heads = key_rows.reshape(batch_size, 2 * length, head_count, head_dim).astype(jnp.float32)
    value_heads = value_rows.reshape(batch_size, 2 * length, head_count, head_dim).astype(
        jnp.float32
    )
    scores = (
        jnp.einsum("bqhd,bkhd->bhqk", query_heads, key_heads) / math.sqrt(head_dim)
        + bias_grid[None]
    )
    scores = jnp.where(allowed[:, None], scores, masked_score)
    highest = lax.stop_gradient(jnp.max(scores, axis=-1, keepdims=True))
    weights = jnp.exp(scores - highest)
    weights = weights / jnp.sum(weights, axis=-1, keepdims=True)
    weights = lax.optimization_barrier(weights.astype(jnp.bfloat16)).astype(jnp.float32)
    mixed_heads = jnp.einsum("bhqk,bkhd->bqhd", weights, value_heads)
    return mixed_heads.reshape(batch_size, length, model_width).astype(jnp.bfloat16)


def taken_logprob(logits, legal_mask, actions):
    legal_flags = legal_mask > 0
    highest = jnp.max(jnp.where(legal_flags, logits, masked_score), axis=-1, keepdims=True)
    partition = jnp.sum(
        jnp.where(legal_flags, jnp.exp(logits - highest), 0.0), axis=-1, keepdims=True
    )
    chosen = lax.broadcasted_iota(jnp.int32, logits.shape, 1) == actions[:, None]
    picked = jnp.sum(jnp.where(chosen, logits, 0.0), axis=-1, keepdims=True)
    return ((picked - highest - jnp.log(partition))[:, 0], chosen, legal_flags)


def bias_table(rel_bias):
    head_count, bias_span = rel_bias.shape
    length = bias_span // 2
    reversed_bias = rel_bias[:, ::-1]
    padded = jnp.concatenate([reversed_bias, jnp.zeros((head_count, length), jnp.float32)], axis=1)
    period = 3 * length
    tiled_rows = jnp.tile(padded, (1, length))[:, : length * (period - 1)]
    shifted = tiled_rows.reshape(head_count, length, period - 1)
    return shifted[:, :, length - 1 : 3 * length - 1]


def contract_rows(left_rows, right_rows):
    return lax.dot_general(
        left_rows, right_rows, (((0,), (0,)), ((), ())), preferred_element_type=jnp.float32
    )


def grad_block(sources):
    pieces = [contract_rows(left_rows, right_rows) for left_rows, right_rows in sources]
    return jnp.concatenate(pieces, axis=1)


def compose_pair(earlier, latter):
    return (latter[0] * earlier[0], latter[1] + latter[0] * earlier[1])


def compose_triple(earlier, latter):
    return (
        latter[0] * earlier[0],
        latter[1] + latter[0] * earlier[1],
        latter[2] + latter[0] * earlier[2],
    )


def mesh_axis_ring(count, step):
    return [(source, (source + step) % count) for source in range(count)]


def reduce_step(blocks, axis, position):
    count, mine = (lax.axis_size(axis), lax.axis_index(axis))

    def block(index):
        return lax.dynamic_index_in_dim(blocks, index, position, keepdims=False)

    total = block(mine).astype(jnp.float32)
    for step in (1, 3, 2):
        sent = block((mine + step) % count).astype(jnp.bfloat16)
        total = total + lax.ppermute(sent, axis, mesh_axis_ring(count, step)).astype(jnp.float32)
    return total


def told_to_all(value, axes):
    count = lax.axis_size(axes)
    row = jnp.zeros((128,), jnp.float32).at[: value.shape[0]].set(value)
    spread = jnp.broadcast_to(row[None], (count, 128)).reshape(-1)
    return lax.all_to_all(spread, axes, 0, 0, tiled=True).reshape(count, 128)


def reduce_grads(pieces, policy):
    core = lax.axis_index("c")
    own, other = [], []
    for piece in pieces:
        own.append(lax.dynamic_slice_in_dim(piece, core * 512, 512, 1))
        other.append(lax.dynamic_slice_in_dim(piece, (1 - core) * 512, 512, 1))
    sent = jnp.concatenate(other, axis=1).astype(jnp.bfloat16)
    got = lax.ppermute(sent, "c", mesh_axis_ring(2, 1))
    paired = jnp.concatenate(own, axis=1) + got.astype(jnp.float32)
    paired = jnp.concatenate([paired, policy], axis=1).astype(jnp.bfloat16)
    cuts = ((0, 768), (768, 1536), (1536, 2176))
    first, second, third = [paired[:, a:b].reshape(4, 4, 4, 16, b - a) for a, b in cuts]
    first, second, third = (
        reduce_step(first, "x", 2),
        reduce_step(second, "y", 1),
        reduce_step(third, "z", 0),
    )
    first, second, third = (
        reduce_step(first, "y", 1),
        reduce_step(second, "z", 0),
        reduce_step(third, "x", 1),
    )
    first, second, third = (
        reduce_step(first, "z", 0),
        reduce_step(second, "x", 0),
        reduce_step(third, "y", 0),
    )
    rows = jnp.concatenate([first, second, third], axis=1).reshape(2, 8, 2176)
    mine = lax.dynamic_index_in_dim(rows, core, 0, keepdims=False)
    theirs = lax.ppermute(
        lax.dynamic_index_in_dim(rows, 1 - core, 0, keepdims=False), "c", mesh_axis_ring(2, 1)
    )
    low = jnp.where(core == 0, mine, theirs)[:, :2048].reshape(8, 4, 1, 512)
    high = jnp.where(core == 0, theirs, mine)[:, :2048].reshape(8, 4, 1, 512)
    main = jnp.concatenate([low, high], axis=2).reshape(8, 4096)
    return jnp.concatenate([main, mine[:, 2048:] + theirs[:, 2048:]], axis=1)


def body(
    states,
    norm_gain,
    w_query,
    w_keyval,
    w_out,
    rel_bias,
    w_policy,
    w_value,
    actions,
    legal_mask,
    rewards,
    episode_end,
    behavior_logprob,
    reg_logprob,
):
    episodes, length, model_width = states.shape
    normed = rms_norm(states, norm_gain)
    memory = passed_along(normed, TIME, 1)
    flat_normed = normed.reshape(episodes * length, model_width)
    queries = (
        jnp.dot(flat_normed, w_query, preferred_element_type=jnp.float32)
        .astype(jnp.bfloat16)
        .reshape(episodes, length, model_width)
    )
    local_kv = (
        jnp.dot(flat_normed, w_keyval, preferred_element_type=jnp.float32)
        .astype(jnp.bfloat16)
        .reshape(episodes, length, 2 * model_width)
    )
    memory_kv = jnp.dot(
        memory.reshape(episodes * length, model_width), w_keyval, preferred_element_type=jnp.float32
    )
    memory_kv = memory_kv.astype(jnp.bfloat16).reshape(episodes, length, 2 * model_width)
    keyvals = jnp.concatenate([memory_kv, local_kv], axis=1)
    key_input = jnp.concatenate([memory, normed], axis=1).reshape(
        episodes * 2 * length, model_width
    )
    bias_grid = bias_table(rel_bias)
    has_memory = jnp.broadcast_to(lax.axis_index(TIME) > 0, (episodes,))
    allowed = make_allowed(has_memory, length)

    def attention_core(query_part, key_part, value_part):
        return attend(query_part, key_part, value_part, bias_grid, allowed)

    attended, pullback = jax.vjp(
        attention_core, queries, keyvals[:, :, :model_width], keyvals[:, :, model_width:]
    )
    flat_att = attended.reshape(episodes * length, model_width)
    projected = jnp.dot(flat_att, w_out, preferred_element_type=jnp.float32)
    hidden = (states.reshape(-1, model_width).astype(jnp.float32) + projected).astype(jnp.bfloat16)
    logits = jnp.dot(hidden, w_policy, preferred_element_type=jnp.float32)
    values = jnp.dot(hidden, w_value, preferred_element_type=jnp.float32).reshape(episodes, length)
    log_flat, chosen, legal_flags = taken_logprob(
        logits, legal_mask.reshape(-1, logits.shape[1]), actions.reshape(-1)
    )
    log_taken = log_flat.reshape(episodes, length)
    clipped = jnp.minimum(1.0, jnp.exp(log_taken - behavior_logprob))
    shaped = rewards.astype(jnp.float32) - reg_weight * (log_taken - reg_logprob)
    carry_on = 1.0 - episode_end.astype(jnp.float32)
    next_local = jnp.concatenate([values[:, 1:], jnp.zeros((episodes, 1), jnp.float32)], axis=1)
    td_error = clipped * (shaped + carry_on * next_local - values)
    trace_decay = carry_on * clipped
    last_col = lax.broadcasted_iota(jnp.int32, (episodes, length), 1) == length - 1
    bridge = jnp.where(last_col, clipped * carry_on, 0.0)
    flipped = (trace_decay[:, ::-1], td_error[:, ::-1], bridge[:, ::-1])
    scanned = lax.associative_scan(compose_triple, flipped, axis=1)
    acc_decay = scanned[0][:, ::-1]
    acc_delta = scanned[1][:, ::-1]
    acc_bridge = scanned[2][:, ::-1]
    told = told_to_all(
        jnp.concatenate([acc_decay[:, 0], acc_delta[:, 0], acc_bridge[:, 0], values[:, 0]]),
        TIME,
    )
    told = told[:, : 4 * episodes].reshape(-1, 4, episodes)
    mine, count = (lax.axis_index(TIME), told.shape[0])
    incoming = jnp.zeros((episodes,), jnp.float32)
    next_value = jnp.zeros((episodes,), jnp.float32)
    for position in range(count - 1, 0, -1):
        gap = told[position, 1] + told[position, 2] * next_value + told[position, 0] * incoming
        incoming = jnp.where(position > mine, gap, incoming)
        next_value = jnp.where(position > mine, told[position, 3], next_value)
    target_gap = acc_delta + acc_bridge * next_value[:, None] + acc_decay * incoming[:, None]
    targets = values + target_gap
    next_targets = jnp.concatenate([targets[:, 1:], (next_value + incoming)[:, None]], axis=1)
    spread = (shaped + carry_on * next_targets - values) * jnp.exp(-behavior_logprob)
    taken_prob = jnp.exp(log_taken)
    adv_taken = jnp.clip((1.0 - taken_prob) * spread, -adv_clip, adv_clip).reshape(-1, 1)
    adv_other = jnp.clip(-taken_prob * spread, -adv_clip, adv_clip).reshape(-1, 1)
    logit_cot = jnp.where(legal_flags, -jnp.where(chosen, adv_taken, adv_other), 0.0).astype(
        jnp.bfloat16
    )
    value_cot = (values - targets).reshape(-1, 1)
    hidden_cot = lax.dot_general(
        logit_cot, w_policy, (((1,), (1,)), ((), ())), preferred_element_type=jnp.float32
    )
    hidden_cot = (hidden_cot + value_cot * w_value.astype(jnp.float32)[None, :]).astype(
        jnp.bfloat16
    )
    att_cot = lax.dot_general(
        hidden_cot, w_out, (((1,), (1,)), ((), ())), preferred_element_type=jnp.float32
    )
    att_cot = att_cot.astype(jnp.bfloat16).reshape(episodes, length, model_width)
    out_sources = ((flat_att, hidden_cot), (hidden, logit_cot))
    grad_query, grad_keys, grad_values = pullback(att_cot)
    grad_kv = jnp.concatenate([grad_keys, grad_values], axis=2).reshape(-1, 2 * model_width)
    in_sources = ((flat_normed, grad_query.reshape(-1, model_width)), (key_input, grad_kv))
    grad_q = contract_rows(*in_sources[0])
    grad_k, grad_v = jnp.split(contract_rows(*in_sources[1]), 2, axis=1)
    grad_o = contract_rows(*out_sources[0])
    grad_p = contract_rows(*out_sources[1])
    raw_rows = reduce_grads((grad_q, grad_k, grad_v, grad_o), grad_p)
    local_squares = jnp.sum(raw_rows * raw_rows)
    grand_total = jnp.sum(told_to_all(local_squares.reshape(1), EVERY))
    entry_count = model_width * raw_rows.shape[1]
    clip_scale = jnp.minimum(1.0, math.sqrt(entry_count) / jnp.sqrt(grand_total + grad_eps))
    return raw_rows * clip_scale


def solution(mesh):
    fine = Mesh(mesh.devices.reshape(4, 4, 4, 2), EVERY)
    return jax.shard_map(
        body,
        mesh=fine,
        in_specs=(
            P("z", TIME, None),
            P(),
            P(),
            P(),
            P(),
            P(),
            P(),
            P(),
            P("z", TIME),
            P("z", TIME, None),
            P("z", TIME),
            P("z", TIME),
            P("z", TIME),
            P("z", TIME),
        ),
        out_specs=P(EVERY, None),
        check_vma=False,
    )
```

```python
import functools
import math

import jax
import jax.numpy as jnp
from jax import lax
from jax.experimental import pallas as pl
from jax.experimental.pallas import tpu as pltpu
from jax.sharding import Mesh
from jax.sharding import PartitionSpec as P

norm_eps = 1e-06
grad_eps = 1e-06
reg_weight = 0.2
adv_clip = 20.0
masked_score = -1e30
EVERY = ("z", "y", "x", "c")
TIME = ("y", "x", "c")

EPS = 6
LEN = 128
ROWS = EPS * LEN
WIDTH = 1024
HEAD = 128
PAIR = 2 * HEAD
ACTS = 128
SEGS = 32
HEADS_ROWS = 144
score_scale = 1.0 / math.sqrt(HEAD)
VMEM_LIMIT = 60 * 1024 * 1024

f32 = jnp.float32
bf16 = jnp.bfloat16


def dot(left, right, left_dim, right_dim):
    return lax.dot_general(
        left, right, (((left_dim,), (right_dim,)), ((), ())), preferred_element_type=f32
    )


def rms_norm(states, norm_gain):
    widened = states.astype(f32)
    spread = jnp.mean(widened * widened, axis=-1, keepdims=True)
    return (widened * lax.rsqrt(spread + norm_eps) * norm_gain).astype(bf16)


def full(shape):
    return pl.BlockSpec(shape, lambda *_: (0,) * len(shape))


def params():
    return pltpu.CompilerParams(
        dimension_semantics=("arbitrary",), vmem_limit_bytes=VMEM_LIMIT
    )


def project_kernel(states_ref, gain_ref, wq_ref, wkv_ref, out_ref, turned_ref, normed_ref):
    step = pl.program_id(0)

    @pl.when(step == 0)
    def _():
        for e in range(EPS):
            rows = pl.ds(e * LEN, LEN)
            normed = rms_norm(states_ref[rows, :], gain_ref[...])
            normed_ref[rows, :] = normed
            turned_ref[:, rows] = normed.T

    @pl.when(step < 2)
    def _():
        out_ref[...] = dot(normed_ref[...], wq_ref[...], 1, 0).astype(bf16)

    @pl.when(step >= 2)
    def _():
        out_ref[...] = dot(normed_ref[...], wkv_ref[...], 1, 0).astype(bf16)


def project(states, gain, w_query, w_keyval):
    return pl.pallas_call(
        project_kernel,
        grid=(6,),
        in_specs=[
            full((ROWS, WIDTH)),
            full((1, WIDTH)),
            pl.BlockSpec((WIDTH, 512), lambda j: (0, jnp.minimum(j, 1))),
            pl.BlockSpec((WIDTH, 512), lambda j: (0, jnp.maximum(j - 2, 0))),
        ],
        out_specs=[
            pl.BlockSpec((ROWS, 512), lambda j: (0, j)),
            full((WIDTH, ROWS)),
        ],
        out_shape=[
            jax.ShapeDtypeStruct((ROWS, 3 * WIDTH), bf16),
            jax.ShapeDtypeStruct((WIDTH, ROWS), bf16),
        ],
        scratch_shapes=[pltpu.VMEM((ROWS, WIDTH), bf16)],
        compiler_params=params(),
        cost_estimate=pl.CostEstimate(
            flops=2 * ROWS * WIDTH * 3 * WIDTH, bytes_accessed=14_000_000, transcendentals=0
        ),
        name="project",
    )(states, gain, w_query, w_keyval)


def action_masks(legal_ref, actions_ref, e):
    legal = legal_ref[e].astype(f32).T > 0.0
    chosen = lax.broadcasted_iota(jnp.int32, (ACTS, LEN), 0) == actions_ref[e : e + 1, :]
    return legal, chosen


def suffix_scan(decay, *sums):
    lane = lax.broadcasted_iota(jnp.int32, decay.shape, 1)
    reach = 1
    while reach < LEN:
        inside = lane < LEN - reach
        ahead = [
            jnp.where(inside, pltpu.roll(part, LEN - reach, 1), 0.0) for part in sums
        ]
        sums = [part + decay * after for part, after in zip(sums, ahead)]
        decay = decay * jnp.where(inside, pltpu.roll(decay, LEN - reach, 1), 1.0)
        reach *= 2
    return (decay, *sums)


def pad_rows(part):
    return jnp.concatenate([part, jnp.zeros((8 - part.shape[0], LEN), f32)], axis=0)


def attend_kernel(
    has_ref,
    mem_ref,
    gain_ref,
    wk_ref,
    wv_ref,
    q_ref,
    kc_ref,
    vc_ref,
    bias_ref,
    wout_ref,
    states_ref,
    wpv_ref,
    legal_ref,
    actions_ref,
    rewards_ref,
    ends_ref,
    behavior_ref,
    reg_ref,
    turned_ref,
    kall_ref,
    vall_ref,
    probs_ref,
    attt_ref,
    hidden_ref,
    stats_ref,
    told_ref,
    memn_ref,
    acc_ref,
    att_ref,
):
    step = pl.program_id(0)

    @pl.when(step == 0)
    def _():
        for e in range(EPS):
            rows = pl.ds(e * LEN, LEN)
            normed = rms_norm(mem_ref[rows, :], gain_ref[...])
            memn_ref[rows, :] = normed
            turned_ref[:, rows] = normed.T

    key_mem = dot(memn_ref[...], wk_ref[...], 1, 0).astype(bf16)
    value_mem = dot(memn_ref[...], wv_ref[...], 1, 0).astype(bf16)
    for e in range(EPS):
        old, new = pl.ds(2 * e * LEN, LEN), pl.ds((2 * e + 1) * LEN, LEN)
        rows = pl.ds(e * LEN, LEN)
        kall_ref[old, :] = key_mem[e * LEN : (e + 1) * LEN]
        vall_ref[old, :] = value_mem[e * LEN : (e + 1) * LEN]
        kall_ref[new, :] = kc_ref[rows, :]
        vall_ref[new, :] = vc_ref[rows, :]

    key_index = lax.broadcasted_iota(jnp.int32, (2 * LEN, LEN), 0)
    query_index = lax.broadcasted_iota(jnp.int32, (2 * LEN, LEN), 1)
    reach = jnp.where(key_index < LEN, LEN * has_ref[0] - 1, LEN + query_index)
    allowed = key_index <= reach
    grids = []
    for h in range(2):
        line = bias_ref[pl.ds(2 * step + h, 1), :]
        grid = pltpu.roll(
            jnp.broadcast_to(line, (LEN, 2 * LEN)), LEN + 1, 1, stride=1, stride_axis=0
        )
        grids.append(jnp.where(allowed, grid.T, masked_score))

    for e in range(EPS):
        rows, both = pl.ds(e * LEN, LEN), pl.ds(2 * e * LEN, 2 * LEN)
        for h in range(2):
            cols = pl.ds(h * HEAD, HEAD)
            scores = dot(kall_ref[both, cols], q_ref[rows, cols], 1, 1)
            scores = jnp.where(allowed, scores * score_scale + grids[h], masked_score)
            highest = jnp.max(scores, axis=0, keepdims=True)
            weights = jnp.exp(scores - highest)
            weights = weights * (1.0 / jnp.sum(weights, axis=0, keepdims=True))
            weights = weights.astype(bf16)
            probs_ref[both, cols] = weights
            att_ref[rows, cols] = dot(weights, vall_ref[both, cols], 0, 0).astype(bf16)

    attt_ref[...] = att_ref[...].T
    part = dot(att_ref[...], wout_ref[...], 1, 0)

    @pl.when(step == 0)
    def _():
        acc_ref[...] = part

    @pl.when(step > 0)
    def _():
        acc_ref[...] += part

    @pl.when(step == 3)
    def _():
        hidden = (states_ref[...].astype(f32) + acc_ref[...]).astype(bf16)
        hidden_ref[...] = hidden
        heads = dot(wpv_ref[...], hidden, 1, 1)
        log_rows, value_rows = [], []
        for e in range(EPS):
            logits = heads[:ACTS, e * LEN : (e + 1) * LEN]
            legal, chosen = action_masks(legal_ref, actions_ref, e)
            highest = jnp.max(jnp.where(legal, logits, masked_score), axis=0, keepdims=True)
            partition = jnp.sum(
                jnp.where(legal, jnp.exp(jnp.where(legal, logits - highest, 0.0)), 0.0),
                axis=0,
                keepdims=True,
            )
            picked = jnp.sum(jnp.where(chosen, logits, 0.0), axis=0, keepdims=True)
            log_rows.append(picked - highest - jnp.log(partition))
            value_rows.append(heads[ACTS : ACTS + 1, e * LEN : (e + 1) * LEN])
        log_taken = jnp.concatenate(log_rows, axis=0)
        values = jnp.concatenate(value_rows, axis=0)
        clipped = jnp.minimum(1.0, jnp.exp(log_taken - behavior_ref[...]))
        shaped = rewards_ref[...].astype(f32) - reg_weight * (log_taken - reg_ref[...])
        carry_on = 1.0 - ends_ref[...].astype(f32)
        last = lax.broadcasted_iota(jnp.int32, (EPS, LEN), 1) == LEN - 1
        next_local = jnp.where(last, 0.0, pltpu.roll(values, LEN - 1, 1))
        td_error = clipped * (shaped + carry_on * next_local - values)
        decay = carry_on * clipped
        bridge = jnp.where(last, decay, 0.0)
        scanned = suffix_scan(decay, td_error, bridge)
        kept = [pad_rows(part) for part in (*scanned, values, log_taken)]
        for index, part in enumerate(kept):
            stats_ref[index] = part
        stacked = jnp.concatenate(kept[:4] + [jnp.zeros((LEN - 32, LEN), f32)], axis=0)
        told_ref[...] = jnp.broadcast_to(stacked.T[0:1, :], (SEGS, LEN))


def attend(has_memory, mem_states, gain, w_keyval, qkv, flipped_bias, w_out, states, wpv, steps):
    legal_mask, actions, rewards, ends, behavior, reg = steps
    small = full((EPS, LEN))
    return pl.pallas_call(
        attend_kernel,
        grid=(4,),
        in_specs=[
            pl.BlockSpec(memory_space=pltpu.SMEM),
            full((ROWS, WIDTH)),
            full((1, WIDTH)),
            pl.BlockSpec((WIDTH, PAIR), lambda g: (0, g)),
            pl.BlockSpec((WIDTH, PAIR), lambda g: (0, 4 + g)),
            pl.BlockSpec((ROWS, PAIR), lambda g: (0, g)),
            pl.BlockSpec((ROWS, PAIR), lambda g: (0, 4 + g)),
            pl.BlockSpec((ROWS, PAIR), lambda g: (0, 8 + g)),
            full((8, 2 * LEN)),
            pl.BlockSpec((PAIR, WIDTH), lambda g: (g, 0)),
            full((ROWS, WIDTH)),
            full((HEADS_ROWS, WIDTH)),
            full((EPS, LEN, ACTS)),
            small,
            small,
            small,
            small,
            small,
        ],
        out_specs=[
            full((WIDTH, ROWS)),
            pl.BlockSpec((2 * ROWS, PAIR), lambda g: (0, g)),
            pl.BlockSpec((2 * ROWS, PAIR), lambda g: (0, g)),
            pl.BlockSpec((2 * ROWS, PAIR), lambda g: (0, g)),
            pl.BlockSpec((PAIR, ROWS), lambda g: (g, 0)),
            full((ROWS, WIDTH)),
            full((5, 8, LEN)),
            full((SEGS, LEN)),
        ],
        out_shape=[
            jax.ShapeDtypeStruct((WIDTH, ROWS), bf16),
            jax.ShapeDtypeStruct((2 * ROWS, WIDTH), bf16),
            jax.ShapeDtypeStruct((2 * ROWS, WIDTH), bf16),
            jax.ShapeDtypeStruct((2 * ROWS, WIDTH), bf16),
            jax.ShapeDtypeStruct((WIDTH, ROWS), bf16),
            jax.ShapeDtypeStruct((ROWS, WIDTH), bf16),
            jax.ShapeDtypeStruct((5, 8, LEN), f32),
            jax.ShapeDtypeStruct((SEGS, LEN), f32),
        ],
        scratch_shapes=[
            pltpu.VMEM((ROWS, WIDTH), bf16),
            pltpu.VMEM((ROWS, WIDTH), f32),
            pltpu.VMEM((ROWS, PAIR), bf16),
        ],
        compiler_params=params(),
        cost_estimate=pl.CostEstimate(
            flops=8_000_000_000, bytes_accessed=30_000_000, transcendentals=1_600_000
        ),
        name="attend",
    )(
        has_memory,
        mem_states,
        gain,
        w_keyval,
        w_keyval,
        qkv,
        qkv,
        qkv,
        flipped_bias,
        w_out,
        states,
        wpv,
        legal_mask,
        actions,
        rewards,
        ends,
        behavior,
        reg,
    )


def cotangent_kernel(
    me_ref,
    told_ref,
    stats_ref,
    rewards_ref,
    ends_ref,
    behavior_ref,
    reg_ref,
    legal_ref,
    actions_ref,
    wpv_ref,
    hidden_ref,
    wout_ref,
    attt_ref,
    attcot_ref,
    gout_ref,
    gpol_ref,
    hcot_ref,
    lcot_ref,
):
    step = pl.program_id(0)

    @pl.when(step == 0)
    def _():
        told = told_ref[...]
        delta, bridge, first = [pltpu.roll(told, LEN - 8 * n, 1) for n in (1, 2, 3)]
        me = me_ref[0]
        incoming = jnp.zeros((1, LEN), f32)
        next_value = jnp.zeros((1, LEN), f32)
        for seg in range(SEGS - 1, 0, -1):
            row = slice(seg, seg + 1)
            gap = delta[row] + bridge[row] * next_value + told[row] * incoming
            incoming = jnp.where(seg > me, gap, incoming)
            next_value = jnp.where(seg > me, first[row], next_value)
        incoming = jnp.broadcast_to(incoming, (LEN, LEN)).T[:EPS]
        next_value = jnp.broadcast_to(next_value, (LEN, LEN)).T[:EPS]

        acc_decay, acc_delta, acc_bridge, values, log_taken = [
            stats_ref[index][:EPS] for index in range(5)
        ]
        behavior = behavior_ref[...]
        shaped = rewards_ref[...].astype(f32) - reg_weight * (log_taken - reg_ref[...])
        carry_on = 1.0 - ends_ref[...].astype(f32)
        target_gap = acc_delta + acc_bridge * next_value + acc_decay * incoming
        targets = values + target_gap
        last = lax.broadcasted_iota(jnp.int32, (EPS, LEN), 1) == LEN - 1
        next_targets = jnp.where(last, next_value + incoming, pltpu.roll(targets, LEN - 1, 1))
        spread = (shaped + carry_on * next_targets - values) * jnp.exp(-behavior)
        taken_prob = jnp.exp(log_taken)
        adv_taken = jnp.clip((1.0 - taken_prob) * spread, -adv_clip, adv_clip)
        adv_other = jnp.clip(-taken_prob * spread, -adv_clip, adv_clip)
        value_cot = jnp.concatenate(
            [values - targets, jnp.zeros((LEN - EPS, LEN), f32)], axis=0
        ).T
        w_policy = wpv_ref[:ACTS, :]
        w_value = wpv_ref[ACTS : ACTS + 16, :].astype(f32)[0:1, :]
        for e in range(EPS):
            legal, chosen = action_masks(legal_ref, actions_ref, e)
            advantage = jnp.where(chosen, adv_taken[e : e + 1], adv_other[e : e + 1])
            logit_cot = jnp.where(legal, -advantage, 0.0)
            lcot_ref[:, pl.ds(e * LEN, LEN)] = logit_cot.astype(bf16)
            cot = dot(logit_cot.T.astype(bf16), w_policy, 1, 0)
            cot = cot + value_cot[:, e : e + 1] * w_value
            hcot_ref[pl.ds(e * LEN, LEN), :] = cot.astype(bf16)
        turned = dot(lcot_ref[...], hidden_ref[...], 1, 0)
        gpol_ref[...] = turned.T.astype(bf16)

    attcot_ref[...] = dot(hcot_ref[...], wout_ref[...], 1, 1).astype(bf16)
    gout_ref[...] = dot(attt_ref[...], hcot_ref[...], 1, 0).astype(bf16)


def cotangents(me, told, stats, steps, wpv, hidden, w_out, attended_turned):
    legal_mask, actions, rewards, ends, behavior, reg = steps
    small = full((EPS, LEN))
    return pl.pallas_call(
        cotangent_kernel,
        grid=(4,),
        in_specs=[
            pl.BlockSpec(memory_space=pltpu.SMEM),
            full((SEGS, LEN)),
            full((5, 8, LEN)),
            small,
            small,
            small,
            small,
            full((EPS, LEN, ACTS)),
            small,
            full((HEADS_ROWS, WIDTH)),
            full((ROWS, WIDTH)),
            pl.BlockSpec((PAIR, WIDTH), lambda n: (n, 0)),
            pl.BlockSpec((PAIR, ROWS), lambda n: (n, 0)),
        ],
        out_specs=[
            pl.BlockSpec((ROWS, PAIR), lambda n: (0, n)),
            pl.BlockSpec((PAIR, WIDTH), lambda n: (n, 0)),
            full((WIDTH, ACTS)),
        ],
        out_shape=[
            jax.ShapeDtypeStruct((ROWS, WIDTH), bf16),
            jax.ShapeDtypeStruct((WIDTH, WIDTH), bf16),
            jax.ShapeDtypeStruct((WIDTH, ACTS), bf16),
        ],
        scratch_shapes=[pltpu.VMEM((ROWS, WIDTH), bf16), pltpu.VMEM((ACTS, ROWS), bf16)],
        compiler_params=params(),
        cost_estimate=pl.CostEstimate(
            flops=4_000_000_000, bytes_accessed=12_000_000, transcendentals=10_000
        ),
        name="cotangents",
    )(
        me,
        told,
        stats,
        rewards,
        ends,
        behavior,
        reg,
        legal_mask,
        actions,
        wpv,
        hidden,
        w_out,
        attended_turned,
    )


def heads_kernel(
    first_ref,
    cot_ref,
    probs_ref,
    q_ref,
    kall_ref,
    vall_ref,
    turned_ref,
    memt_ref,
    gq_ref,
    gk_ref,
    gv_ref,
    new_ref,
    old_ref,
):
    for e in range(EPS):
        rows, both = pl.ds(e * LEN, LEN), pl.ds(2 * e * LEN, 2 * LEN)
        for h in range(2):
            cols = pl.ds(h * HEAD, HEAD)
            cot = cot_ref[rows, cols]
            weights = probs_ref[both, cols]
            wide = weights.astype(f32)
            weight_cot = dot(vall_ref[both, cols], cot, 1, 1).astype(bf16).astype(f32)
            product = wide * weight_cot
            inner = jnp.sum(product, axis=0, keepdims=True)
            score_cot = ((product - wide * inner) * score_scale).astype(bf16)
            value_grad = dot(weights, cot, 1, 0).astype(bf16)
            key_grad = dot(score_cot, q_ref[rows, cols], 1, 0).astype(bf16)
            query_grad = dot(score_cot, kall_ref[both, cols], 0, 0).astype(bf16)
            new_ref[rows, pl.ds(h * HEAD, HEAD)] = query_grad
            new_ref[rows, pl.ds(PAIR + h * HEAD, HEAD)] = key_grad[LEN:]
            new_ref[rows, pl.ds(2 * PAIR + h * HEAD, HEAD)] = value_grad[LEN:]
            old_ref[rows, pl.ds(h * HEAD, HEAD)] = key_grad[:LEN]
            old_ref[rows, pl.ds(PAIR + h * HEAD, HEAD)] = value_grad[:LEN]
    for half in range(2):
        part = pl.ds(half * 512, 512)
        fresh = dot(turned_ref[part, :], new_ref[...], 1, 0)
        stale = dot(memt_ref[part, :], old_ref[...], 1, 0)
        gq_ref[part, :] = fresh[:, :PAIR].astype(bf16)
        gk_ref[part, :] = (fresh[:, PAIR : 2 * PAIR] + stale[:, :PAIR]).astype(bf16)
        gv_ref[part, :] = (fresh[:, 2 * PAIR :] + stale[:, PAIR:]).astype(bf16)


def heads_backward(first, att_cot, probs, qkv, kall, vall, turned, mem_turned):
    grad = pl.BlockSpec((WIDTH, PAIR), lambda g, first: (0, g))
    return pl.pallas_call(
        heads_kernel,
        grid_spec=pltpu.PrefetchScalarGridSpec(
            num_scalar_prefetch=1,
            grid=(2,),
            in_specs=[
                pl.BlockSpec((ROWS, PAIR), lambda g, first: (0, first[0] + g)),
                pl.BlockSpec((2 * ROWS, PAIR), lambda g, first: (0, first[0] + g)),
                pl.BlockSpec((ROWS, PAIR), lambda g, first: (0, first[0] + g)),
                pl.BlockSpec((2 * ROWS, PAIR), lambda g, first: (0, first[0] + g)),
                pl.BlockSpec((2 * ROWS, PAIR), lambda g, first: (0, first[0] + g)),
                full((WIDTH, ROWS)),
                full((WIDTH, ROWS)),
            ],
            out_specs=[grad, grad, grad],
            scratch_shapes=[
                pltpu.VMEM((ROWS, 3 * PAIR), bf16),
                pltpu.VMEM((ROWS, 2 * PAIR), bf16),
            ],
        ),
        out_shape=[jax.ShapeDtypeStruct((WIDTH, 2 * PAIR), bf16)] * 3,
        compiler_params=params(),
        cost_estimate=pl.CostEstimate(
            flops=5_000_000_000, bytes_accessed=14_000_000, transcendentals=0
        ),
        name="heads_backward",
    )(first, att_cot, probs, qkv, kall, vall, turned, mem_turned)


def ring(count, step):
    return [(source, (source + step) % count) for source in range(count)]


def reduce_step(blocks, axis, position):
    count, mine = (lax.axis_size(axis), lax.axis_index(axis))

    def block(index):
        return lax.dynamic_index_in_dim(blocks, index, position, keepdims=False)

    total = block(mine).astype(f32)
    for step in (1, 3, 2):
        sent = block((mine + step) % count).astype(bf16)
        total = total + lax.ppermute(sent, axis, ring(count, step)).astype(f32)
    return total


def reduce_over_chips(paired):
    cuts = ((0, 768), (768, 1536), (1536, 2176))
    first, second, third = [paired[:, a:b].reshape(4, 4, 4, 16, b - a) for a, b in cuts]
    first, second, third = (
        reduce_step(first, "x", 2),
        reduce_step(second, "y", 1),
        reduce_step(third, "z", 0),
    )
    first, second, third = (
        reduce_step(first, "y", 1),
        reduce_step(second, "z", 0),
        reduce_step(third, "x", 1),
    )
    first, second, third = (
        reduce_step(first, "z", 0),
        reduce_step(second, "x", 0),
        reduce_step(third, "y", 0),
    )
    return jnp.concatenate([first, second, third], axis=1)


def gather_columns(rows, core):
    rows = rows.reshape(2, 8, 2176)
    mine = lax.dynamic_index_in_dim(rows, core, 0, keepdims=False)
    theirs = lax.ppermute(
        lax.dynamic_index_in_dim(rows, 1 - core, 0, keepdims=False), "c", ring(2, 1)
    )
    low = jnp.where(core == 0, mine, theirs)[:, :2048].reshape(8, 4, 1, 512)
    high = jnp.where(core == 0, theirs, mine)[:, :2048].reshape(8, 4, 1, 512)
    main = jnp.concatenate([low, high], axis=2).reshape(8, 4096)
    return jnp.concatenate([main, mine[:, 2048:] + theirs[:, 2048:]], axis=1)


def body(
    states,
    norm_gain,
    w_query,
    w_keyval,
    w_out,
    rel_bias,
    w_policy,
    w_value,
    actions,
    legal_mask,
    rewards,
    episode_end,
    behavior_logprob,
    reg_logprob,
):
    core, segment = lax.axis_index("c"), lax.axis_index(TIME)
    states = states.reshape(ROWS, WIDTH)
    links = [(source, source + 1) for source in range(SEGS - 1)]
    mem_states = lax.ppermute(states, TIME, links)
    gain = norm_gain.reshape(1, WIDTH)
    wpv = jnp.concatenate(
        [w_policy.T, w_value[None], jnp.zeros((HEADS_ROWS - ACTS - 1, WIDTH), bf16)], axis=0
    )
    steps = (legal_mask, actions, rewards, episode_end, behavior_logprob, reg_logprob)

    qkv, turned = project(states, gain, w_query, w_keyval)
    has_memory = (segment > 0).astype(jnp.int32).reshape(1)
    mem_turned, kall, vall, probs, att_turned, hidden, stats, told = attend(
        has_memory, mem_states, gain, w_keyval, qkv, rel_bias[:, ::-1], w_out, states, wpv, steps
    )
    told = lax.all_to_all(told, TIME, 0, 0, tiled=True)
    att_cot, grad_out, grad_policy = cotangents(
        segment.reshape(1), told, stats, steps, wpv, hidden, w_out, att_turned
    )
    backward = functools.partial(
        heads_backward,
        att_cot=att_cot,
        probs=probs,
        qkv=qkv,
        kall=kall,
        vall=vall,
        turned=turned,
        mem_turned=mem_turned,
    )
    out_own = lax.dynamic_slice_in_dim(grad_out, core * 512, 512, 1)
    out_other = lax.dynamic_slice_in_dim(grad_out, (1 - core) * 512, 512, 1)
    others = backward(first=(2 * (1 - core)).reshape(1))
    got = [lax.ppermute(part, "c", ring(2, 1)) for part in (*others, out_other)]
    owned = backward(first=(2 * core).reshape(1))
    paired = [
        (own.astype(f32) + part.astype(f32)).astype(bf16)
        for own, part in zip((*owned, out_own), got)
    ]
    rows = reduce_over_chips(jnp.concatenate([*paired, grad_policy], axis=1))
    raw_rows = gather_columns(rows, core)
    squares = jnp.sum(raw_rows * raw_rows)
    spread = jnp.zeros((128, 128), f32).at[:, 0].set(squares)
    grand_total = jnp.sum(lax.all_to_all(spread, EVERY, 0, 0, tiled=True))
    entry_count = WIDTH * raw_rows.shape[1]
    clip_scale = jnp.minimum(1.0, math.sqrt(entry_count) / jnp.sqrt(grand_total + grad_eps))
    return raw_rows * clip_scale


def solution(mesh):
    fine = Mesh(mesh.devices.reshape(4, 4, 4, 2), EVERY)
    by_step = P("z", TIME)
    return jax.shard_map(
        body,
        mesh=fine,
        in_specs=(
            P("z", TIME, None),
            P(),
            P(),
            P(),
            P(),
            P(),
            P(),
            P(),
            by_step,
            P("z", TIME, None),
            by_step,
            by_step,
            by_step,
            by_step,
        ),
        out_specs=P(EVERY, None),
        check_vma=False,
    )
```

```python
import functools
import math

import jax
import jax.numpy as jnp
from jax import lax
from jax.experimental import pallas as pl
from jax.experimental.pallas import tpu as pltpu
from jax.sharding import Mesh
from jax.sharding import PartitionSpec as P


norm_eps = 1e-06
grad_eps = 1e-06
reg_weight = 0.2
adv_clip = 20.0
masked_score = -1e30
EVERY = ("z", "y", "x", "c")
TIME = ("y", "x", "c")


EPS = 6
LEN = 128
ROWS = EPS * LEN
WIDTH = 1024
HEAD = 128
PAIR = 2 * HEAD
HALF = 4 * HEAD
ACTS = 128
SEGS = 32
score_scale = 1.0 / math.sqrt(HEAD)
VMEM_LIMIT = 67_043_328

f32 = jnp.float32
bf16 = jnp.bfloat16


def dot(left, right, left_dim, right_dim):
    return lax.dot_general(
        left, right, (((left_dim,), (right_dim,)), ((), ())), preferred_element_type=f32
    )


def rms_norm(states, norm_gain):
    widened = states.astype(f32)
    spread = jnp.mean(widened * widened, axis=-1, keepdims=True)
    return (widened * lax.rsqrt(spread + norm_eps) * norm_gain).astype(bf16)


def full(shape):
    return pl.BlockSpec(shape, lambda *_: (0,) * len(shape))


def params():
    return pltpu.CompilerParams(
        dimension_semantics=("arbitrary",), vmem_limit_bytes=VMEM_LIMIT
    )


def project_kernel(states_ref, gain_ref, wq_ref, wkv_ref, out_ref, turned_ref, normed_ref):
    step = pl.program_id(0)

    @pl.when(step == 0)
    def _():
        for e in range(EPS):
            rows = pl.ds(e * LEN, LEN)
            normed = rms_norm(states_ref[rows, :], gain_ref[...])
            normed_ref[rows, :] = normed
            turned_ref[:, rows] = normed.T

    @pl.when(step < 2)
    def _():
        out_ref[...] = dot(normed_ref[...], wq_ref[...], 1, 0).astype(bf16)

    @pl.when(step >= 2)
    def _():
        out_ref[...] = dot(normed_ref[...], wkv_ref[...], 1, 0).astype(bf16)


def project(states, gain, w_query, w_keyval):
    return pl.pallas_call(
        project_kernel,
        grid=(6,),
        in_specs=[
            full((ROWS, WIDTH)),
            full((1, WIDTH)),
            pl.BlockSpec((WIDTH, 512), lambda j: (0, jnp.minimum(j, 1))),
            pl.BlockSpec((WIDTH, 512), lambda j: (0, jnp.maximum(j - 2, 0))),
        ],
        out_specs=[
            pl.BlockSpec((ROWS, 512), lambda j: (0, j)),
            full((WIDTH, ROWS)),
        ],
        out_shape=[
            jax.ShapeDtypeStruct((ROWS, 3 * WIDTH), bf16),
            jax.ShapeDtypeStruct((WIDTH, ROWS), bf16),
        ],
        scratch_shapes=[pltpu.VMEM((ROWS, WIDTH), bf16)],
        compiler_params=params(),
        cost_estimate=pl.CostEstimate(
            flops=2 * ROWS * WIDTH * 3 * WIDTH, bytes_accessed=14_000_000, transcendentals=0
        ),
        name="project",
    )(states, gain, w_query, w_keyval)


def action_masks(legal_ref, actions_ref, block, e):
    legal = legal_ref[block].astype(f32).T > 0.0
    chosen = lax.broadcasted_iota(jnp.int32, (ACTS, LEN), 0) == actions_ref[e : e + 1, :]
    return legal, chosen


def by_head(rows):
    zeros = jnp.zeros((LEN, HEAD), rows.dtype)
    upper = jnp.concatenate([rows[:, :HEAD], zeros], axis=1)
    lower = jnp.concatenate([zeros, rows[:, HEAD:]], axis=1)
    return jnp.concatenate([upper, lower], axis=0)


def suffix_scan(decay, *sums):
    lane = lax.broadcasted_iota(jnp.int32, decay.shape, 1)
    reach = 1
    while reach < LEN:
        inside = lane < LEN - reach
        ahead = [
            jnp.where(inside, pltpu.roll(part, LEN - reach, 1), 0.0) for part in sums
        ]
        sums = [part + decay * after for part, after in zip(sums, ahead)]
        decay = decay * jnp.where(inside, pltpu.roll(decay, LEN - reach, 1), 1.0)
        reach *= 2
    return (decay, *sums)


def pad_rows(part):
    return jnp.concatenate([part, jnp.zeros((8 - part.shape[0], LEN), f32)], axis=0)


def attend_kernel(
    has_ref,
    mem_ref,
    gain_ref,
    wk_ref,
    wv_ref,
    q_ref,
    kc_ref,
    vc_ref,
    bias_ref,
    wout_ref,
    states_hbm,
    wpolicy_ref,
    wvalue_ref,
    legal_hbm,
    actions_ref,
    rewards_ref,
    ends_ref,
    behavior_ref,
    reg_ref,
    turned_hbm,
    kmem_ref,
    vmem_ref,
    probs_ref,
    attt_ref,
    hidden_hbm,
    stats_ref,
    told_ref,
    memn_ref,
    acc_ref,
    att_ref,
    states_ref,
    legal_ref,
    turned_ref,
    hidden_ref,
    sem_ref,
):
    step = pl.program_id(0)
    states_copy = pltpu.make_async_copy(states_hbm, states_ref, sem_ref.at[0])
    legal_copy = pltpu.make_async_copy(legal_hbm, legal_ref, sem_ref.at[1])
    turned_copy = pltpu.make_async_copy(turned_ref, turned_hbm, sem_ref.at[2])
    hidden_copy = pltpu.make_async_copy(hidden_ref, hidden_hbm, sem_ref.at[3])

    @pl.when(step == 0)
    def _():
        for e in range(EPS):
            rows = pl.ds(e * LEN, LEN)
            normed = rms_norm(mem_ref[rows, :], gain_ref[...])
            memn_ref[rows, :] = normed
            turned_ref[:, rows] = normed.T
        states_copy.start()
        legal_copy.start()
        turned_copy.start()

    kmem_ref[...] = dot(memn_ref[...], wk_ref[...], 1, 0).astype(bf16)
    vmem_ref[...] = dot(memn_ref[...], wv_ref[...], 1, 0).astype(bf16)

    key_index = lax.broadcasted_iota(jnp.int32, (2 * LEN, LEN), 0)
    query_index = lax.broadcasted_iota(jnp.int32, (2 * LEN, LEN), 1)
    reach = jnp.where(key_index < LEN, LEN * has_ref[0] - 1, LEN + query_index)
    allowed = key_index <= reach
    grids = []
    for h in range(2):
        line = bias_ref[pl.ds(2 * step + h, 1), :]
        grid = pltpu.roll(
            jnp.broadcast_to(line, (2 * LEN, 2 * LEN)), LEN, 1, stride=1, stride_axis=0
        )
        grids.append(grid[:, :LEN])

    for e in range(EPS):
        rows = pl.ds(e * LEN, LEN)
        both = pl.ds(2 * e * LEN, 2 * LEN)
        keys = jnp.concatenate([kmem_ref[rows, :], kc_ref[rows, :]], axis=0)
        values = jnp.concatenate([vmem_ref[rows, :], vc_ref[rows, :]], axis=0)
        products = dot(keys, by_head(q_ref[rows, :]), 1, 1)
        for h in range(2):
            cols = pl.ds(h * HEAD, HEAD)
            scores = products[:, h * LEN : (h + 1) * LEN]
            scores = jnp.where(allowed, scores * score_scale + grids[h], masked_score)
            highest = jnp.max(scores, axis=0, keepdims=True)
            weights = jnp.exp(scores - highest)
            weights = weights * (1.0 / jnp.sum(weights, axis=0, keepdims=True))
            weights = weights.astype(bf16)
            probs_ref[both, cols] = weights
            mixed = dot(weights, values[:, h * HEAD : (h + 1) * HEAD], 0, 0)
            att_ref[rows, cols] = mixed.astype(bf16)

    attt_ref[...] = att_ref[...].T
    part = dot(att_ref[...], wout_ref[...], 1, 0)

    @pl.when(step == 0)
    def _():
        acc_ref[...] = part

    @pl.when(step > 0)
    def _():
        acc_ref[...] += part

    @pl.when(step == 3)
    def _():
        states_copy.wait()
        hidden = (states_ref[...].astype(f32) + acc_ref[...]).astype(bf16)
        hidden_ref[...] = hidden
        hidden_copy.start()
        legal_copy.wait()
        all_logits = dot(wpolicy_ref[...].T, hidden, 1, 1)
        all_values = dot(jnp.broadcast_to(wvalue_ref[...], (16, WIDTH)), hidden, 1, 1)
        log_rows, value_rows = [], []
        for e in range(EPS):
            logits = all_logits[:, e * LEN : (e + 1) * LEN]
            legal, chosen = action_masks(legal_ref, actions_ref, e, e)
            highest = jnp.max(jnp.where(legal, logits, masked_score), axis=0, keepdims=True)
            partition = jnp.sum(
                jnp.where(legal, jnp.exp(jnp.where(legal, logits - highest, 0.0)), 0.0),
                axis=0,
                keepdims=True,
            )
            picked = jnp.sum(jnp.where(chosen, logits, 0.0), axis=0, keepdims=True)
            log_rows.append(picked - highest - jnp.log(partition))
            value_rows.append(all_values[0:1, e * LEN : (e + 1) * LEN])
        log_taken = jnp.concatenate(log_rows, axis=0)
        values = jnp.concatenate(value_rows, axis=0)
        clipped = jnp.minimum(1.0, jnp.exp(log_taken - behavior_ref[...]))
        shaped = rewards_ref[...].astype(f32) - reg_weight * (log_taken - reg_ref[...])
        carry_on = 1.0 - ends_ref[...].astype(f32)
        last = lax.broadcasted_iota(jnp.int32, (EPS, LEN), 1) == LEN - 1
        next_local = jnp.where(last, 0.0, pltpu.roll(values, LEN - 1, 1))
        td_error = clipped * (shaped + carry_on * next_local - values)
        decay = carry_on * clipped
        bridge = jnp.where(last, decay, 0.0)
        kept = [*suffix_scan(decay, td_error, bridge), values, log_taken]
        kept = [pad_rows(part) for part in kept]
        for index, part in enumerate(kept):
            stats_ref[index] = part
        stacked = jnp.concatenate(kept[:4] + [jnp.zeros((LEN - 32, LEN), f32)], axis=0)
        told_ref[...] = jnp.broadcast_to(stacked.T[0:1, :], (SEGS, LEN))
        turned_copy.wait()
        hidden_copy.wait()


def attend(has_memory, mem_states, gain, w_keyval, qkv, weights, states, steps):
    w_out, rel_bias, w_policy, w_value = weights
    legal_mask, actions, rewards, ends, behavior, reg = steps
    small = full((EPS, LEN))
    inputs = [
        has_memory,
        mem_states,
        gain,
        w_keyval,
        w_keyval,
        qkv,
        qkv,
        qkv,
        rel_bias,
        w_out,
        states,
        w_policy,
        w_value,
        legal_mask,
        actions,
        rewards,
        ends,
        behavior,
        reg,
    ]
    in_specs = [
        pl.BlockSpec(memory_space=pltpu.SMEM),
        full((ROWS, WIDTH)),
        full((1, WIDTH)),
        pl.BlockSpec((WIDTH, PAIR), lambda g: (0, g)),
        pl.BlockSpec((WIDTH, PAIR), lambda g: (0, 4 + g)),
        pl.BlockSpec((ROWS, PAIR), lambda g: (0, g)),
        pl.BlockSpec((ROWS, PAIR), lambda g: (0, 4 + g)),
        pl.BlockSpec((ROWS, PAIR), lambda g: (0, 8 + g)),
        full((8, 2 * LEN)),
        pl.BlockSpec((PAIR, WIDTH), lambda g: (g, 0)),
        pl.BlockSpec(memory_space=pl.ANY),
        full((WIDTH, ACTS)),
        full((1, WIDTH)),
        pl.BlockSpec(memory_space=pl.ANY),
        small,
        small,
        small,
        small,
        small,
    ]
    out_specs = [
        pl.BlockSpec(memory_space=pl.ANY),
        pl.BlockSpec((ROWS, PAIR), lambda g: (0, g)),
        pl.BlockSpec((ROWS, PAIR), lambda g: (0, g)),
        pl.BlockSpec((2 * ROWS, PAIR), lambda g: (0, g)),
        pl.BlockSpec((PAIR, ROWS), lambda g: (g, 0)),
        pl.BlockSpec(memory_space=pl.ANY),
        full((5, 8, LEN)),
        full((SEGS, LEN)),
    ]
    out_shape = [
        jax.ShapeDtypeStruct((WIDTH, ROWS), bf16),
        jax.ShapeDtypeStruct((ROWS, WIDTH), bf16),
        jax.ShapeDtypeStruct((ROWS, WIDTH), bf16),
        jax.ShapeDtypeStruct((2 * ROWS, WIDTH), bf16),
        jax.ShapeDtypeStruct((WIDTH, ROWS), bf16),
        jax.ShapeDtypeStruct((ROWS, WIDTH), bf16),
        jax.ShapeDtypeStruct((5, 8, LEN), f32),
        jax.ShapeDtypeStruct((SEGS, LEN), f32),
    ]
    return pl.pallas_call(
        attend_kernel,
        grid=(4,),
        in_specs=in_specs,
        out_specs=out_specs,
        out_shape=out_shape,
        scratch_shapes=[
            pltpu.VMEM((ROWS, WIDTH), bf16),
            pltpu.VMEM((ROWS, WIDTH), f32),
            pltpu.VMEM((ROWS, PAIR), bf16),
            pltpu.VMEM((ROWS, WIDTH), bf16),
            pltpu.VMEM((EPS, LEN, ACTS), jnp.int32),
            pltpu.VMEM((WIDTH, ROWS), bf16),
            pltpu.VMEM((ROWS, WIDTH), bf16),
            pltpu.SemaphoreType.DMA((4,)),
        ],
        compiler_params=params(),
        cost_estimate=pl.CostEstimate(
            flops=4_000_000_000, bytes_accessed=15_000_000, transcendentals=800_000
        ),
        name="attend",
    )(*inputs)


def cotangent_kernel(
    me_ref,
    told_ref,
    stats_ref,
    rewards_ref,
    ends_ref,
    behavior_ref,
    reg_ref,
    legal_ref,
    actions_ref,
    wpolicy_ref,
    wvalue_ref,
    hidden_ref,
    wout_ref,
    attt_ref,
    attcot_ref,
    own_ref,
    other_ref,
    gpol_ref,
    hcot_ref,
    lcot_ref,
):
    step = pl.program_id(0)

    @pl.when(step == 0)
    def _():
        told = told_ref[...]
        delta, bridge, first = [pltpu.roll(told, LEN - 8 * n, 1) for n in (1, 2, 3)]
        me = me_ref[0]
        incoming = jnp.zeros((1, LEN), f32)
        next_value = jnp.zeros((1, LEN), f32)
        for seg in range(SEGS - 1, 0, -1):
            row = slice(seg, seg + 1)
            gap = delta[row] + bridge[row] * next_value + told[row] * incoming
            incoming = jnp.where(seg > me, gap, incoming)
            next_value = jnp.where(seg > me, first[row], next_value)
        incoming = jnp.broadcast_to(incoming, (LEN, LEN)).T[:EPS]
        next_value = jnp.broadcast_to(next_value, (LEN, LEN)).T[:EPS]

        acc_decay, acc_delta, acc_bridge, values, log_taken = [
            stats_ref[index][:EPS] for index in range(5)
        ]
        behavior = behavior_ref[...]
        shaped = rewards_ref[...].astype(f32) - reg_weight * (log_taken - reg_ref[...])
        carry_on = 1.0 - ends_ref[...].astype(f32)
        target_gap = acc_delta + acc_bridge * next_value + acc_decay * incoming
        targets = values + target_gap
        last = lax.broadcasted_iota(jnp.int32, (EPS, LEN), 1) == LEN - 1
        next_targets = jnp.where(last, next_value + incoming, pltpu.roll(targets, LEN - 1, 1))
        spread = (shaped + carry_on * next_targets - values) * jnp.exp(-behavior)
        taken_prob = jnp.exp(log_taken)
        adv_taken = jnp.clip((1.0 - taken_prob) * spread, -adv_clip, adv_clip)
        adv_other = jnp.clip(-taken_prob * spread, -adv_clip, adv_clip)
        value_cot = jnp.concatenate(
            [values - targets, jnp.zeros((LEN - EPS, LEN), f32)], axis=0
        ).T
        w_policy = wpolicy_ref[...].T
        w_value = wvalue_ref[...].astype(f32)
        for e in range(EPS):
            legal, chosen = action_masks(legal_ref, actions_ref, e, e)
            advantage = jnp.where(chosen, adv_taken[e : e + 1], adv_other[e : e + 1])
            logit_cot = jnp.where(legal, -advantage, 0.0)
            lcot_ref[:, pl.ds(e * LEN, LEN)] = logit_cot.astype(bf16)
            cot = dot(logit_cot.T.astype(bf16), w_policy, 1, 0)
            cot = cot + value_cot[:, e : e + 1] * w_value
            hcot_ref[pl.ds(e * LEN, LEN), :] = cot.astype(bf16)
        gpol_ref[...] = dot(lcot_ref[...], hidden_ref[...], 1, 0).T.astype(bf16)

    attcot_ref[...] = dot(hcot_ref[...], wout_ref[...], 1, 1).astype(bf16)
    core = lax.rem(me_ref[0], 2)
    for half, grad_ref in ((core, own_ref), (1 - core, other_ref)):
        cols = pl.ds(pl.multiple_of(half * HALF, HALF), HALF)
        grad_ref[...] = dot(attt_ref[...], hcot_ref[:, cols], 1, 0).astype(bf16)


def cotangents(me, told, stats, steps, weights, hidden, attended_turned):
    w_out, _, w_policy, w_value = weights
    legal_mask, actions, rewards, ends, behavior, reg = steps
    small = full((EPS, LEN))
    return pl.pallas_call(
        cotangent_kernel,
        grid=(4,),
        in_specs=[
            pl.BlockSpec(memory_space=pltpu.SMEM),
            full((SEGS, LEN)),
            full((5, 8, LEN)),
            small,
            small,
            small,
            small,
            full((EPS, LEN, ACTS)),
            small,
            full((WIDTH, ACTS)),
            full((1, WIDTH)),
            full((ROWS, WIDTH)),
            pl.BlockSpec((PAIR, WIDTH), lambda n: (n, 0)),
            pl.BlockSpec((PAIR, ROWS), lambda n: (n, 0)),
        ],
        out_specs=[
            pl.BlockSpec((ROWS, PAIR), lambda n: (0, n)),
            pl.BlockSpec((PAIR, HALF), lambda n: (n, 0)),
            pl.BlockSpec((PAIR, HALF), lambda n: (n, 0)),
            full((WIDTH, ACTS)),
        ],
        out_shape=[
            jax.ShapeDtypeStruct((ROWS, WIDTH), bf16),
            jax.ShapeDtypeStruct((WIDTH, HALF), bf16),
            jax.ShapeDtypeStruct((WIDTH, HALF), bf16),
            jax.ShapeDtypeStruct((WIDTH, ACTS), bf16),
        ],
        scratch_shapes=[
            pltpu.VMEM((ROWS, WIDTH), bf16),
            pltpu.VMEM((ACTS, ROWS), bf16),
        ],
        compiler_params=params(),
        cost_estimate=pl.CostEstimate(
            flops=4_000_000_000, bytes_accessed=12_000_000, transcendentals=10_000
        ),
        name="cotangents",
    )(
        me,
        told,
        stats,
        rewards,
        ends,
        behavior,
        reg,
        legal_mask,
        actions,
        w_policy,
        w_value,
        hidden,
        w_out,
        attended_turned,
    )


def heads_kernel(
    first_ref,
    cot_ref,
    probs_ref,
    q_ref,
    kmem_ref,
    kc_ref,
    vmem_ref,
    vc_ref,
    turned_ref,
    memt_ref,
    grad_ref,
    new_ref,
    old_ref,
):
    for e in range(EPS):
        rows, both = pl.ds(e * LEN, LEN), pl.ds(2 * e * LEN, 2 * LEN)
        cot = by_head(cot_ref[rows, :])
        weights = probs_ref[both, :]
        wide = weights.astype(f32)
        keys = jnp.concatenate([kmem_ref[rows, :], kc_ref[rows, :]], axis=0)
        values = jnp.concatenate([vmem_ref[rows, :], vc_ref[rows, :]], axis=0)
        weight_cot = dot(values, cot, 1, 1).astype(bf16).astype(f32)
        product = wide * weight_cot
        inner = jnp.sum(product, axis=0, keepdims=True)
        score_cot = ((product - wide * inner) * score_scale).astype(bf16)
        value_grad = dot(weights, cot, 1, 0).astype(bf16)
        key_grad = dot(score_cot, by_head(q_ref[rows, :]), 1, 0).astype(bf16)
        for h in range(2):
            cols = pl.ds(h * HEAD, HEAD)
            new_ref[rows, cols] = dot(
                score_cot[:, h * LEN : (h + 1) * LEN],
                keys[:, h * HEAD : (h + 1) * HEAD],
                0,
                0,
            ).astype(bf16)
        new_ref[rows, pl.ds(PAIR, PAIR)] = key_grad[LEN:]
        new_ref[rows, pl.ds(2 * PAIR, PAIR)] = value_grad[LEN:]
        old_ref[rows, pl.ds(0, PAIR)] = key_grad[:LEN]
        old_ref[rows, pl.ds(PAIR, PAIR)] = value_grad[:LEN]
    for half in range(2):
        part = pl.ds(half * 512, 512)
        fresh = dot(turned_ref[part, :], new_ref[...], 1, 0)
        stale = dot(memt_ref[part, :], old_ref[...], 1, 0)
        grad_ref[part, pl.ds(0, PAIR)] = fresh[:, :PAIR].astype(bf16)
        grad_ref[part, pl.ds(PAIR, 2 * PAIR)] = (fresh[:, PAIR:] + stale).astype(bf16)


def heads_backward(first, att_cot, probs, qkv, kmem, vmem, turned, mem_turned):
    return pl.pallas_call(
        heads_kernel,
        grid_spec=pltpu.PrefetchScalarGridSpec(
            num_scalar_prefetch=1,
            grid=(2,),
            in_specs=[
                pl.BlockSpec((ROWS, PAIR), lambda g, first: (0, first[0] + g)),
                pl.BlockSpec((2 * ROWS, PAIR), lambda g, first: (0, first[0] + g)),
                pl.BlockSpec((ROWS, PAIR), lambda g, first: (0, first[0] + g)),
                pl.BlockSpec((ROWS, PAIR), lambda g, first: (0, first[0] + g)),
                pl.BlockSpec((ROWS, PAIR), lambda g, first: (0, 4 + first[0] + g)),
                pl.BlockSpec((ROWS, PAIR), lambda g, first: (0, first[0] + g)),
                pl.BlockSpec((ROWS, PAIR), lambda g, first: (0, 8 + first[0] + g)),
                full((WIDTH, ROWS)),
                full((WIDTH, ROWS)),
            ],
            out_specs=pl.BlockSpec((WIDTH, 3 * PAIR), lambda g, first: (0, g)),
            scratch_shapes=[
                pltpu.VMEM((ROWS, 3 * PAIR), bf16),
                pltpu.VMEM((ROWS, 2 * PAIR), bf16),
            ],
        ),
        out_shape=jax.ShapeDtypeStruct((WIDTH, 6 * PAIR), bf16),
        compiler_params=params(),
        cost_estimate=pl.CostEstimate(
            flops=5_000_000_000, bytes_accessed=14_000_000, transcendentals=0
        ),
        name="heads_backward",
    )(first, att_cot, probs, qkv, kmem, qkv, vmem, qkv, turned, mem_turned)


COLS_C = HALF + ACTS


def pair_kernel(place_ref, own_ref, got_ref, oown_ref, ogot_ref, pol_ref, *out_refs):
    a_refs, b_refs, c_refs = out_refs[:4], out_refs[4:8], out_refs[8:]
    step = pl.program_id(0)

    def paired(index, cols):
        left = own_ref[0, index, :, :, cols].astype(f32)
        return (left + got_ref[0, index, :, :, cols].astype(f32)).astype(bf16)

    def paired_out(index, cols):
        left = oown_ref[0, index, :, :, cols].astype(f32)
        return (left + ogot_ref[0, index, :, :, cols].astype(f32)).astype(bf16)

    for j in range(4):
        x = lax.rem(place_ref[0] + j, 4)
        y = lax.rem(place_ref[1] + j, 4)
        for p in range(4):
            for n, half in enumerate((pl.ds(0, PAIR), pl.ds(3 * PAIR, PAIR))):
                value = own_ref[0, p, x, :, half].astype(f32) + got_ref[0, p, x, :, half].astype(f32)
                a_refs[j][0, p, :, pl.ds(n * PAIR, PAIR)] = value.astype(bf16)
            half = pl.ds(0, PAIR)
            value = oown_ref[0, p, x, :, half].astype(f32) + ogot_ref[0, p, x, :, half].astype(f32)
            a_refs[j][0, p, :, pl.ds(2 * PAIR, PAIR)] = value.astype(bf16)
        for n in range(2):
            b_refs[j][0, :, :, pl.ds(n * PAIR, PAIR)] = paired(y, pl.ds((3 * n + 1) * PAIR, PAIR))
        b_refs[j][0, :, :, pl.ds(2 * PAIR, PAIR)] = paired_out(y, pl.ds(PAIR, PAIR))

        @pl.when(step == j)
        def _(j=j):
            for p in range(4):
                for n in range(2):
                    c_refs[j][p, :, :, pl.ds(n * PAIR, PAIR)] = paired(
                        p, pl.ds((3 * n + 2) * PAIR, PAIR)
                    )
                c_refs[j][p, :, :, pl.ds(HALF, ACTS)] = pol_ref[0, p]


def pair_sum(place, own, got, out_own, out_got, policy):
    def layer(cols):
        return pl.BlockSpec(
            (1, 4, 4, 16, cols), lambda j, place: (lax.rem(place[2] + j, 4), 0, 0, 0, 0)
        )

    group = pl.BlockSpec((1, 4, 16, 768), lambda j, place: (lax.rem(place[2] + j, 4), 0, 0, 0))
    last = pl.BlockSpec((4, 4, 16, COLS_C), lambda j, place: (0, 0, 0, 0))
    parts = [part.reshape(4, 4, 4, 16, -1) for part in (own, got, out_own, out_got, policy)]
    shapes = [jax.ShapeDtypeStruct((4, 4, 16, 768), bf16)] * 8
    shapes += [jax.ShapeDtypeStruct((4, 4, 16, COLS_C), bf16)] * 4
    out = pl.pallas_call(
        pair_kernel,
        grid_spec=pltpu.PrefetchScalarGridSpec(
            num_scalar_prefetch=1,
            grid=(4,),
            in_specs=[layer(part.shape[-1]) for part in parts],
            out_specs=[group] * 8 + [last] * 4,
        ),
        out_shape=shapes,
        compiler_params=params(),
        name="pair_sum",
    )(place, *parts)
    return out[:4], out[4:8], out[8:]


def ring(count, step):
    return [(source, (source + step) % count) for source in range(count)]


def swapped(part):
    return lax.ppermute(part, "c", ring(2, 1))


def hop_sum(blocks, axis):
    total = blocks[0].astype(f32)
    for step in (2, 1, 3):
        got = lax.ppermute(blocks[step].astype(bf16), axis, ring(4, step))
        total = total + got.astype(f32)
    return total


def further(total, position, axis):
    mine = lax.axis_index(axis)
    return [
        lax.dynamic_index_in_dim(total, (mine + step) % 4, position, keepdims=False)
        for step in range(4)
    ]


def sum_over_devices(own, got, out_own, out_got, policy):
    core = lax.axis_index("c")
    place = jnp.stack([lax.axis_index(axis) for axis in "xyz"])
    a_blocks, b_blocks, c_blocks = pair_sum(place, own, got, out_own, out_got, policy)
    a = hop_sum(a_blocks, "x")
    b = hop_sum(b_blocks, "y")
    c = hop_sum(c_blocks, "z")
    ac = [
        jnp.concatenate([left.astype(bf16), right.astype(bf16)], axis=2)
        for left, right in zip(further(a, 1, "y"), further(c, 0, "y"))
    ]
    ac = hop_sum(ac, "y")
    b = hop_sum(further(b, 1, "x"), "x")
    ab = jnp.concatenate([ac[:, :, :768], b], axis=2).astype(bf16).reshape(8, 8, 1536)
    ab = lax.all_to_all(ab, ("z", "c"), 0, 0, tiled=True).reshape(4, 2, 8, 1536)
    ab = jnp.sum(ab.astype(f32), axis=0)
    c = hop_sum(further(ac[:, :, 768:], 0, "x"), "x").reshape(2, 8, COLS_C)
    mine = lax.dynamic_index_in_dim(c, core, 0, keepdims=False)
    theirs = swapped(lax.dynamic_index_in_dim(c, 1 - core, 0, keepdims=False))
    c = jnp.stack([jnp.where(core == 0, mine, theirs), jnp.where(core == 0, theirs, mine)])
    out = jnp.concatenate([ab[:, :, 512:768], ab[:, :, 1280:]], axis=2)
    square = [ab[:, :, :512], ab[:, :, 768:1280], c[:, :, :HALF], out]
    columns = [part.transpose(1, 0, 2).reshape(8, WIDTH) for part in square]
    return jnp.concatenate([*columns, c[0, :, HALF:] + c[1, :, HALF:]], axis=1)


def body(
    states,
    norm_gain,
    w_query,
    w_keyval,
    w_out,
    rel_bias,
    w_policy,
    w_value,
    actions,
    legal_mask,
    rewards,
    episode_end,
    behavior_logprob,
    reg_logprob,
):
    core, segment = lax.axis_index("c"), lax.axis_index(TIME)
    states = states.reshape(ROWS, WIDTH)
    links = [(source, source + 1) for source in range(SEGS - 1)]
    mem_states = lax.ppermute(states, TIME, links)
    gain = norm_gain.reshape(1, WIDTH)
    steps = (legal_mask, actions, rewards, episode_end, behavior_logprob, reg_logprob)
    weights = (w_out, rel_bias, w_policy, w_value.reshape(1, WIDTH))

    qkv, turned = project(states, gain, w_query, w_keyval)
    has_memory = (segment > 0).astype(jnp.int32).reshape(1)
    mem_turned, kmem, vmem, probs, att_turned, hidden, stats, told = attend(
        has_memory, mem_states, gain, w_keyval, qkv, weights, states, steps
    )
    told = lax.all_to_all(told, TIME, 0, 0, tiled=True)
    att_cot, out_own, out_other, grad_policy = cotangents(
        segment.reshape(1), told, stats, steps, weights, hidden, att_turned
    )
    out_got = swapped(out_other)
    backward = functools.partial(
        heads_backward,
        att_cot=att_cot,
        probs=probs,
        qkv=qkv,
        kmem=kmem,
        vmem=vmem,
        turned=turned,
        mem_turned=mem_turned,
    )
    got = swapped(backward(first=(2 * (1 - core)).reshape(1)))
    owned = backward(first=(2 * core).reshape(1))
    raw_rows = sum_over_devices(owned, got, out_own, out_got, grad_policy)
    squares = jnp.sum(raw_rows * raw_rows)
    spread = jnp.broadcast_to(squares * (1.0 / 128.0), (128, 128))
    grand_total = jnp.sum(lax.all_to_all(spread, EVERY, 0, 0, tiled=True))
    entry_count = WIDTH * raw_rows.shape[1]
    clip_scale = jnp.minimum(1.0, math.sqrt(entry_count) / jnp.sqrt(grand_total + grad_eps))
    return raw_rows * clip_scale


def solution(mesh):
    fine = Mesh(mesh.devices.reshape(4, 4, 4, 2), EVERY)
    by_step = P("z", TIME)
    return jax.shard_map(
        body,
        mesh=fine,
        in_specs=(
            P("z", TIME, None),
            P(),
            P(),
            P(),
            P(),
            P(),
            P(),
            P(),
            by_step,
            P("z", TIME, None),
            by_step,
            by_step,
            by_step,
            by_step,
        ),
        out_specs=P(EVERY, None),
        check_vma=False,
    )
```

```python
import functools
import math

import jax
import jax.numpy as jnp
from jax import lax
from jax.experimental import pallas as pl
from jax.experimental.pallas import tpu as pltpu
from jax.sharding import Mesh
from jax.sharding import PartitionSpec as P


norm_eps = 1e-06
grad_eps = 1e-06
reg_weight = 0.2
adv_clip = 20.0
masked_score = -1e30
EVERY = ("z", "y", "x", "c")
TIME = ("y", "x", "c")


EPS = 6
LEN = 128
ROWS = EPS * LEN
WIDTH = 1024
HEAD = 128
PAIR = 2 * HEAD
HALF = 4 * HEAD
ACTS = 128
SEGS = 32
score_scale = 1.0 / math.sqrt(HEAD)
VMEM_LIMIT = 67_043_328

f32 = jnp.float32
bf16 = jnp.bfloat16


def dot(left, right, left_dim, right_dim):
    return lax.dot_general(
        left, right, (((left_dim,), (right_dim,)), ((), ())), preferred_element_type=f32
    )


def rms_norm(states, norm_gain):
    widened = states.astype(f32)
    spread = jnp.mean(widened * widened, axis=-1, keepdims=True)
    return (widened * lax.rsqrt(spread + norm_eps) * norm_gain).astype(bf16)


def full(shape):
    return pl.BlockSpec(shape, lambda *_: (0,) * len(shape))


def params():
    return pltpu.CompilerParams(
        dimension_semantics=("arbitrary",), vmem_limit_bytes=VMEM_LIMIT
    )


def project_kernel(states_ref, gain_ref, wq_ref, wkv_ref, out_ref, turned_ref, normed_ref):
    step = pl.program_id(0)

    @pl.when(step == 0)
    def _():
        for e in range(EPS):
            rows = pl.ds(e * LEN, LEN)
            normed = rms_norm(states_ref[rows, :], gain_ref[...])
            normed_ref[rows, :] = normed
            turned_ref[:, rows] = normed.T

    def put(columns):
        out_ref[0] = columns[:, :PAIR]
        out_ref[1] = columns[:, PAIR:]

    @pl.when(step < 2)
    def _():
        put(dot(normed_ref[...], wq_ref[...], 1, 0).astype(bf16))

    @pl.when(step >= 2)
    def _():
        put(dot(normed_ref[...], wkv_ref[...], 1, 0).astype(bf16))


def project(states, gain, w_query, w_keyval):
    return pl.pallas_call(
        project_kernel,
        grid=(6,),
        in_specs=[
            full((ROWS, WIDTH)),
            full((1, WIDTH)),
            pl.BlockSpec((WIDTH, 512), lambda j: (0, jnp.minimum(j, 1))),
            pl.BlockSpec((WIDTH, 512), lambda j: (0, jnp.maximum(j - 2, 0))),
        ],
        out_specs=[
            pl.BlockSpec((2, ROWS, PAIR), lambda j: (j, 0, 0)),
            full((WIDTH, ROWS)),
        ],
        out_shape=[
            jax.ShapeDtypeStruct((12, ROWS, PAIR), bf16),
            jax.ShapeDtypeStruct((WIDTH, ROWS), bf16),
        ],
        scratch_shapes=[pltpu.VMEM((ROWS, WIDTH), bf16)],
        compiler_params=params(),
        cost_estimate=pl.CostEstimate(
            flops=2 * ROWS * WIDTH * 3 * WIDTH, bytes_accessed=14_000_000, transcendentals=0
        ),
        name="project",
    )(states, gain, w_query, w_keyval)


def action_masks(legal_ref, actions_ref, block, e):
    legal = legal_ref[block].astype(f32).T > 0.0
    chosen = lax.broadcasted_iota(jnp.int32, (ACTS, LEN), 0) == actions_ref[e : e + 1, :]
    return legal, chosen


def by_head(rows):
    zeros = jnp.zeros((LEN, HEAD), rows.dtype)
    upper = jnp.concatenate([rows[:, :HEAD], zeros], axis=1)
    lower = jnp.concatenate([zeros, rows[:, HEAD:]], axis=1)
    return jnp.concatenate([upper, lower], axis=0)


def suffix_scan(decay, *sums):
    lane = lax.broadcasted_iota(jnp.int32, decay.shape, 1)
    reach = 1
    while reach < LEN:
        inside = lane < LEN - reach
        ahead = [
            jnp.where(inside, pltpu.roll(part, LEN - reach, 1), 0.0) for part in sums
        ]
        sums = [part + decay * after for part, after in zip(sums, ahead)]
        decay = decay * jnp.where(inside, pltpu.roll(decay, LEN - reach, 1), 1.0)
        reach *= 2
    return (decay, *sums)


def pad_rows(part):
    return jnp.concatenate([part, jnp.zeros((8 - part.shape[0], LEN), f32)], axis=0)


def attend_kernel(
    has_ref,
    mem_ref,
    gain_ref,
    wk_ref,
    wv_ref,
    q_ref,
    kc_ref,
    vc_ref,
    bias_ref,
    wout_ref,
    states_hbm,
    wpolicy_ref,
    wvalue_ref,
    legal_hbm,
    actions_ref,
    rewards_ref,
    ends_ref,
    behavior_ref,
    reg_ref,
    turned_hbm,
    kmem_ref,
    vmem_ref,
    probs_ref,
    attt_ref,
    hidden_hbm,
    stats_ref,
    told_ref,
    memn_ref,
    acc_ref,
    att_ref,
    states_ref,
    legal_ref,
    turned_ref,
    hidden_ref,
    sem_ref,
):
    step = pl.program_id(0)
    states_copy = pltpu.make_async_copy(states_hbm, states_ref, sem_ref.at[0])
    legal_copy = pltpu.make_async_copy(legal_hbm, legal_ref, sem_ref.at[1])
    turned_copy = pltpu.make_async_copy(turned_ref, turned_hbm, sem_ref.at[2])
    hidden_copy = pltpu.make_async_copy(hidden_ref, hidden_hbm, sem_ref.at[3])

    @pl.when(step == 0)
    def _():
        for e in range(EPS):
            rows = pl.ds(e * LEN, LEN)
            normed = rms_norm(mem_ref[rows, :], gain_ref[...])
            memn_ref[rows, :] = normed
            turned_ref[:, rows] = normed.T
        states_copy.start()
        legal_copy.start()
        turned_copy.start()

    kmem_ref[...] = dot(memn_ref[...], wk_ref[...], 1, 0).astype(bf16)
    vmem_ref[...] = dot(memn_ref[...], wv_ref[...], 1, 0).astype(bf16)

    key_index = lax.broadcasted_iota(jnp.int32, (2 * LEN, LEN), 0)
    query_index = lax.broadcasted_iota(jnp.int32, (2 * LEN, LEN), 1)
    reach = jnp.where(key_index < LEN, LEN * has_ref[0] - 1, LEN + query_index)
    allowed = key_index <= reach
    grids = []
    for h in range(2):
        line = bias_ref[pl.ds(2 * step + h, 1), :]
        grid = pltpu.roll(
            jnp.broadcast_to(line, (2 * LEN, 2 * LEN)), LEN, 1, stride=1, stride_axis=0
        )
        grids.append(grid[:, :LEN])

    for e in range(EPS):
        rows = pl.ds(e * LEN, LEN)
        both = pl.ds(2 * e * LEN, 2 * LEN)
        keys = jnp.concatenate([kmem_ref[rows, :], kc_ref[rows, :]], axis=0)
        values = jnp.concatenate([vmem_ref[rows, :], vc_ref[rows, :]], axis=0)
        products = dot(keys, by_head(q_ref[rows, :]), 1, 1)
        for h in range(2):
            cols = pl.ds(h * HEAD, HEAD)
            scores = products[:, h * LEN : (h + 1) * LEN]
            scores = jnp.where(allowed, scores * score_scale + grids[h], masked_score)
            highest = jnp.max(scores, axis=0, keepdims=True)
            weights = jnp.exp(scores - highest)
            weights = weights * (1.0 / jnp.sum(weights, axis=0, keepdims=True))
            weights = weights.astype(bf16)
            probs_ref[both, cols] = weights
            mixed = dot(weights, values[:, h * HEAD : (h + 1) * HEAD], 0, 0)
            att_ref[rows, cols] = mixed.astype(bf16)

    attt_ref[...] = att_ref[...].T
    part = dot(att_ref[...], wout_ref[...], 1, 0)

    @pl.when(step == 0)
    def _():
        acc_ref[...] = part

    @pl.when(step > 0)
    def _():
        acc_ref[...] += part

    @pl.when(step == 3)
    def _():
        states_copy.wait()
        hidden = (states_ref[...].astype(f32) + acc_ref[...]).astype(bf16)
        hidden_ref[...] = hidden
        hidden_copy.start()
        legal_copy.wait()
        all_logits = dot(wpolicy_ref[...].T, hidden, 1, 1)
        all_values = dot(jnp.broadcast_to(wvalue_ref[...], (16, WIDTH)), hidden, 1, 1)
        log_rows, value_rows = [], []
        for e in range(EPS):
            logits = all_logits[:, e * LEN : (e + 1) * LEN]
            legal, chosen = action_masks(legal_ref, actions_ref, e, e)
            highest = jnp.max(jnp.where(legal, logits, masked_score), axis=0, keepdims=True)
            partition = jnp.sum(
                jnp.where(legal, jnp.exp(jnp.where(legal, logits - highest, 0.0)), 0.0),
                axis=0,
                keepdims=True,
            )
            picked = jnp.sum(jnp.where(chosen, logits, 0.0), axis=0, keepdims=True)
            log_rows.append(picked - highest - jnp.log(partition))
            value_rows.append(all_values[0:1, e * LEN : (e + 1) * LEN])
        log_taken = jnp.concatenate(log_rows, axis=0)
        values = jnp.concatenate(value_rows, axis=0)
        clipped = jnp.minimum(1.0, jnp.exp(log_taken - behavior_ref[...]))
        shaped = rewards_ref[...].astype(f32) - reg_weight * (log_taken - reg_ref[...])
        carry_on = 1.0 - ends_ref[...].astype(f32)
        last = lax.broadcasted_iota(jnp.int32, (EPS, LEN), 1) == LEN - 1
        next_local = jnp.where(last, 0.0, pltpu.roll(values, LEN - 1, 1))
        td_error = clipped * (shaped + carry_on * next_local - values)
        decay = carry_on * clipped
        bridge = jnp.where(last, decay, 0.0)
        kept = [*suffix_scan(decay, td_error, bridge), values, log_taken]
        kept = [pad_rows(part) for part in kept]
        for index, part in enumerate(kept):
            stats_ref[index] = part
        stacked = jnp.concatenate(kept[:4] + [jnp.zeros((LEN - 32, LEN), f32)], axis=0)
        told_ref[...] = jnp.broadcast_to(stacked.T[0:1, :], (SEGS, LEN))
        turned_copy.wait()
        hidden_copy.wait()


def attend(has_memory, mem_states, gain, w_keyval, qkv, weights, states, steps):
    w_out, rel_bias, w_policy, w_value = weights
    legal_mask, actions, rewards, ends, behavior, reg = steps
    small = full((EPS, LEN))
    inputs = [
        has_memory,
        mem_states,
        gain,
        w_keyval,
        w_keyval,
        qkv,
        qkv,
        qkv,
        rel_bias,
        w_out,
        states,
        w_policy,
        w_value,
        legal_mask,
        actions,
        rewards,
        ends,
        behavior,
        reg,
    ]
    in_specs = [
        pl.BlockSpec(memory_space=pltpu.SMEM),
        full((ROWS, WIDTH)),
        full((1, WIDTH)),
        pl.BlockSpec((WIDTH, PAIR), lambda g: (0, g)),
        pl.BlockSpec((WIDTH, PAIR), lambda g: (0, 4 + g)),
        pl.BlockSpec((None, ROWS, PAIR), lambda g: (g, 0, 0)),
        pl.BlockSpec((None, ROWS, PAIR), lambda g: (4 + g, 0, 0)),
        pl.BlockSpec((None, ROWS, PAIR), lambda g: (8 + g, 0, 0)),
        full((8, 2 * LEN)),
        pl.BlockSpec((PAIR, WIDTH), lambda g: (g, 0)),
        pl.BlockSpec(memory_space=pl.ANY),
        full((WIDTH, ACTS)),
        full((1, WIDTH)),
        pl.BlockSpec(memory_space=pl.ANY),
        small,
        small,
        small,
        small,
        small,
    ]
    out_specs = [
        pl.BlockSpec(memory_space=pl.ANY),
        pl.BlockSpec((None, ROWS, PAIR), lambda g: (g, 0, 0)),
        pl.BlockSpec((None, ROWS, PAIR), lambda g: (g, 0, 0)),
        pl.BlockSpec((None, 2 * ROWS, PAIR), lambda g: (g, 0, 0)),
        pl.BlockSpec((PAIR, ROWS), lambda g: (g, 0)),
        pl.BlockSpec(memory_space=pl.ANY),
        full((5, 8, LEN)),
        full((SEGS, LEN)),
    ]
    out_shape = [
        jax.ShapeDtypeStruct((WIDTH, ROWS), bf16),
        jax.ShapeDtypeStruct((4, ROWS, PAIR), bf16),
        jax.ShapeDtypeStruct((4, ROWS, PAIR), bf16),
        jax.ShapeDtypeStruct((4, 2 * ROWS, PAIR), bf16),
        jax.ShapeDtypeStruct((WIDTH, ROWS), bf16),
        jax.ShapeDtypeStruct((ROWS, WIDTH), bf16),
        jax.ShapeDtypeStruct((5, 8, LEN), f32),
        jax.ShapeDtypeStruct((SEGS, LEN), f32),
    ]
    return pl.pallas_call(
        attend_kernel,
        grid=(4,),
        in_specs=in_specs,
        out_specs=out_specs,
        out_shape=out_shape,
        scratch_shapes=[
            pltpu.VMEM((ROWS, WIDTH), bf16),
            pltpu.VMEM((ROWS, WIDTH), f32),
            pltpu.VMEM((ROWS, PAIR), bf16),
            pltpu.VMEM((ROWS, WIDTH), bf16),
            pltpu.VMEM((EPS, LEN, ACTS), jnp.int32),
            pltpu.VMEM((WIDTH, ROWS), bf16),
            pltpu.VMEM((ROWS, WIDTH), bf16),
            pltpu.SemaphoreType.DMA((4,)),
        ],
        compiler_params=params(),
        cost_estimate=pl.CostEstimate(
            flops=4_000_000_000, bytes_accessed=15_000_000, transcendentals=800_000
        ),
        name="attend",
    )(*inputs)


def cotangent_kernel(
    me_ref,
    told_ref,
    stats_ref,
    rewards_ref,
    ends_ref,
    behavior_ref,
    reg_ref,
    legal_ref,
    actions_ref,
    wpolicy_ref,
    wvalue_ref,
    hidden_ref,
    wout_ref,
    attt_ref,
    attcot_ref,
    own_ref,
    other_ref,
    gpol_ref,
    hcot_ref,
    lcot_ref,
):
    step = pl.program_id(0)

    @pl.when(step == 0)
    def _():
        told = told_ref[...]
        delta, bridge, first = [pltpu.roll(told, LEN - 8 * n, 1) for n in (1, 2, 3)]
        me = me_ref[0]
        incoming = jnp.zeros((1, LEN), f32)
        next_value = jnp.zeros((1, LEN), f32)
        for seg in range(SEGS - 1, 0, -1):
            row = slice(seg, seg + 1)
            gap = delta[row] + bridge[row] * next_value + told[row] * incoming
            incoming = jnp.where(seg > me, gap, incoming)
            next_value = jnp.where(seg > me, first[row], next_value)
        incoming = jnp.broadcast_to(incoming, (LEN, LEN)).T[:EPS]
        next_value = jnp.broadcast_to(next_value, (LEN, LEN)).T[:EPS]

        acc_decay, acc_delta, acc_bridge, values, log_taken = [
            stats_ref[index][:EPS] for index in range(5)
        ]
        behavior = behavior_ref[...]
        shaped = rewards_ref[...].astype(f32) - reg_weight * (log_taken - reg_ref[...])
        carry_on = 1.0 - ends_ref[...].astype(f32)
        target_gap = acc_delta + acc_bridge * next_value + acc_decay * incoming
        targets = values + target_gap
        last = lax.broadcasted_iota(jnp.int32, (EPS, LEN), 1) == LEN - 1
        next_targets = jnp.where(last, next_value + incoming, pltpu.roll(targets, LEN - 1, 1))
        spread = (shaped + carry_on * next_targets - values) * jnp.exp(-behavior)
        taken_prob = jnp.exp(log_taken)
        adv_taken = jnp.clip((1.0 - taken_prob) * spread, -adv_clip, adv_clip)
        adv_other = jnp.clip(-taken_prob * spread, -adv_clip, adv_clip)
        value_cot = jnp.concatenate(
            [values - targets, jnp.zeros((LEN - EPS, LEN), f32)], axis=0
        ).T
        w_policy = wpolicy_ref[...].T
        w_value = wvalue_ref[...].astype(f32)
        for e in range(EPS):
            legal, chosen = action_masks(legal_ref, actions_ref, e, e)
            advantage = jnp.where(chosen, adv_taken[e : e + 1], adv_other[e : e + 1])
            logit_cot = jnp.where(legal, -advantage, 0.0)
            lcot_ref[:, pl.ds(e * LEN, LEN)] = logit_cot.astype(bf16)
            cot = dot(logit_cot.T.astype(bf16), w_policy, 1, 0)
            cot = cot + value_cot[:, e : e + 1] * w_value
            hcot_ref[pl.ds(e * LEN, LEN), :] = cot.astype(bf16)
        gpol_ref[...] = dot(lcot_ref[...], hidden_ref[...], 1, 0).T.astype(bf16)

    attcot_ref[...] = dot(hcot_ref[...], wout_ref[...], 1, 1).astype(bf16)
    core = lax.rem(me_ref[0], 2)
    for half, grad_ref in ((core, own_ref), (1 - core, other_ref)):
        cols = pl.ds(pl.multiple_of(half * HALF, HALF), HALF)
        grad_ref[...] = dot(attt_ref[...], hcot_ref[:, cols], 1, 0).astype(bf16)


def cotangents(me, told, stats, steps, weights, hidden, attended_turned):
    w_out, _, w_policy, w_value = weights
    legal_mask, actions, rewards, ends, behavior, reg = steps
    small = full((EPS, LEN))
    return pl.pallas_call(
        cotangent_kernel,
        grid=(4,),
        in_specs=[
            pl.BlockSpec(memory_space=pltpu.SMEM),
            full((SEGS, LEN)),
            full((5, 8, LEN)),
            small,
            small,
            small,
            small,
            full((EPS, LEN, ACTS)),
            small,
            full((WIDTH, ACTS)),
            full((1, WIDTH)),
            full((ROWS, WIDTH)),
            pl.BlockSpec((PAIR, WIDTH), lambda n: (n, 0)),
            pl.BlockSpec((PAIR, ROWS), lambda n: (n, 0)),
        ],
        out_specs=[
            pl.BlockSpec((None, ROWS, PAIR), lambda n: (n, 0, 0)),
            pl.BlockSpec((PAIR, HALF), lambda n: (n, 0)),
            pl.BlockSpec((PAIR, HALF), lambda n: (n, 0)),
            full((WIDTH, ACTS)),
        ],
        out_shape=[
            jax.ShapeDtypeStruct((4, ROWS, PAIR), bf16),
            jax.ShapeDtypeStruct((WIDTH, HALF), bf16),
            jax.ShapeDtypeStruct((WIDTH, HALF), bf16),
            jax.ShapeDtypeStruct((WIDTH, ACTS), bf16),
        ],
        scratch_shapes=[
            pltpu.VMEM((ROWS, WIDTH), bf16),
            pltpu.VMEM((ACTS, ROWS), bf16),
        ],
        compiler_params=params(),
        cost_estimate=pl.CostEstimate(
            flops=4_000_000_000, bytes_accessed=12_000_000, transcendentals=10_000
        ),
        name="cotangents",
    )(
        me,
        told,
        stats,
        rewards,
        ends,
        behavior,
        reg,
        legal_mask,
        actions,
        w_policy,
        w_value,
        hidden,
        w_out,
        attended_turned,
    )


def heads_kernel(
    first_ref,
    cot_ref,
    probs_ref,
    q_ref,
    kmem_ref,
    kc_ref,
    vmem_ref,
    vc_ref,
    turned_ref,
    memt_ref,
    grad_ref,
    new_ref,
    old_ref,
):
    for e in range(EPS):
        rows, both = pl.ds(e * LEN, LEN), pl.ds(2 * e * LEN, 2 * LEN)
        cot = by_head(cot_ref[rows, :])
        weights = probs_ref[both, :]
        wide = weights.astype(f32)
        keys = jnp.concatenate([kmem_ref[rows, :], kc_ref[rows, :]], axis=0)
        values = jnp.concatenate([vmem_ref[rows, :], vc_ref[rows, :]], axis=0)
        weight_cot = dot(values, cot, 1, 1).astype(bf16).astype(f32)
        product = wide * weight_cot
        inner = jnp.sum(product, axis=0, keepdims=True)
        score_cot = ((product - wide * inner) * score_scale).astype(bf16)
        value_grad = dot(weights, cot, 1, 0).astype(bf16)
        key_grad = dot(score_cot, by_head(q_ref[rows, :]), 1, 0).astype(bf16)
        for h in range(2):
            cols = pl.ds(h * HEAD, HEAD)
            new_ref[rows, cols] = dot(
                score_cot[:, h * LEN : (h + 1) * LEN],
                keys[:, h * HEAD : (h + 1) * HEAD],
                0,
                0,
            ).astype(bf16)
        new_ref[rows, pl.ds(PAIR, PAIR)] = key_grad[LEN:]
        new_ref[rows, pl.ds(2 * PAIR, PAIR)] = value_grad[LEN:]
        old_ref[rows, pl.ds(0, PAIR)] = key_grad[:LEN]
        old_ref[rows, pl.ds(PAIR, PAIR)] = value_grad[:LEN]
    for half in range(2):
        part = pl.ds(half * 512, 512)
        fresh = dot(turned_ref[part, :], new_ref[...], 1, 0)
        stale = dot(memt_ref[part, :], old_ref[...], 1, 0)
        grad_ref[part, pl.ds(0, PAIR)] = fresh[:, :PAIR].astype(bf16)
        grad_ref[part, pl.ds(PAIR, 2 * PAIR)] = (fresh[:, PAIR:] + stale).astype(bf16)


def heads_backward(first, att_cot, probs, qkv, kmem, vmem, turned, mem_turned):
    return pl.pallas_call(
        heads_kernel,
        grid_spec=pltpu.PrefetchScalarGridSpec(
            num_scalar_prefetch=1,
            grid=(2,),
            in_specs=[
                pl.BlockSpec((None, ROWS, PAIR), lambda g, first: (first[0] + g, 0, 0)),
                pl.BlockSpec((None, 2 * ROWS, PAIR), lambda g, first: (first[0] + g, 0, 0)),
                pl.BlockSpec((None, ROWS, PAIR), lambda g, first: (first[0] + g, 0, 0)),
                pl.BlockSpec((None, ROWS, PAIR), lambda g, first: (first[0] + g, 0, 0)),
                pl.BlockSpec((None, ROWS, PAIR), lambda g, first: (4 + first[0] + g, 0, 0)),
                pl.BlockSpec((None, ROWS, PAIR), lambda g, first: (first[0] + g, 0, 0)),
                pl.BlockSpec((None, ROWS, PAIR), lambda g, first: (8 + first[0] + g, 0, 0)),
                full((WIDTH, ROWS)),
                full((WIDTH, ROWS)),
            ],
            out_specs=pl.BlockSpec((WIDTH, 3 * PAIR), lambda g, first: (0, g)),
            scratch_shapes=[
                pltpu.VMEM((ROWS, 3 * PAIR), bf16),
                pltpu.VMEM((ROWS, 2 * PAIR), bf16),
            ],
        ),
        out_shape=jax.ShapeDtypeStruct((WIDTH, 6 * PAIR), bf16),
        compiler_params=params(),
        cost_estimate=pl.CostEstimate(
            flops=5_000_000_000, bytes_accessed=14_000_000, transcendentals=0
        ),
        name="heads_backward",
    )(first, att_cot, probs, qkv, kmem, qkv, vmem, qkv, turned, mem_turned)


COLS_C = HALF + ACTS


def pair_kernel(place_ref, own_ref, got_ref, oown_ref, ogot_ref, pol_ref, *out_refs):
    a_refs, b_refs, c_refs = out_refs[:4], out_refs[4:8], out_refs[8:]
    step = pl.program_id(0)

    def paired(index, cols):
        left = own_ref[0, index, :, :, cols].astype(f32)
        return (left + got_ref[0, index, :, :, cols].astype(f32)).astype(bf16)

    def paired_out(index, cols):
        left = oown_ref[0, index, :, :, cols].astype(f32)
        return (left + ogot_ref[0, index, :, :, cols].astype(f32)).astype(bf16)

    for j in range(4):
        x = lax.rem(place_ref[0] + j, 4)
        y = lax.rem(place_ref[1] + j, 4)
        for p in range(4):
            for n, half in enumerate((pl.ds(0, PAIR), pl.ds(3 * PAIR, PAIR))):
                value = own_ref[0, p, x, :, half].astype(f32) + got_ref[0, p, x, :, half].astype(f32)
                a_refs[j][0, p, :, pl.ds(n * PAIR, PAIR)] = value.astype(bf16)
            half = pl.ds(0, PAIR)
            value = oown_ref[0, p, x, :, half].astype(f32) + ogot_ref[0, p, x, :, half].astype(f32)
            a_refs[j][0, p, :, pl.ds(2 * PAIR, PAIR)] = value.astype(bf16)
        for n in range(2):
            b_refs[j][0, :, :, pl.ds(n * PAIR, PAIR)] = paired(y, pl.ds((3 * n + 1) * PAIR, PAIR))
        b_refs[j][0, :, :, pl.ds(2 * PAIR, PAIR)] = paired_out(y, pl.ds(PAIR, PAIR))

        @pl.when(step == j)
        def _(j=j):
            for p in range(4):
                for n in range(2):
                    c_refs[j][p, :, :, pl.ds(n * PAIR, PAIR)] = paired(
                        p, pl.ds((3 * n + 2) * PAIR, PAIR)
                    )
                c_refs[j][p, :, :, pl.ds(HALF, ACTS)] = pol_ref[0, p]


def pair_sum(place, own, got, out_own, out_got, policy):
    def layer(cols):
        return pl.BlockSpec(
            (1, 4, 4, 16, cols), lambda j, place: (lax.rem(place[2] + j, 4), 0, 0, 0, 0)
        )

    group = pl.BlockSpec((1, 4, 16, 768), lambda j, place: (lax.rem(place[2] + j, 4), 0, 0, 0))
    last = pl.BlockSpec((4, 4, 16, COLS_C), lambda j, place: (0, 0, 0, 0))
    parts = [part.reshape(4, 4, 4, 16, -1) for part in (own, got, out_own, out_got, policy)]
    shapes = [jax.ShapeDtypeStruct((4, 4, 16, 768), bf16)] * 8
    shapes += [jax.ShapeDtypeStruct((4, 4, 16, COLS_C), bf16)] * 4
    out = pl.pallas_call(
        pair_kernel,
        grid_spec=pltpu.PrefetchScalarGridSpec(
            num_scalar_prefetch=1,
            grid=(4,),
            in_specs=[layer(part.shape[-1]) for part in parts],
            out_specs=[group] * 8 + [last] * 4,
        ),
        out_shape=shapes,
        compiler_params=params(),
        name="pair_sum",
    )(place, *parts)
    return out[:4], out[4:8], out[8:]


def ring(count, step):
    return [(source, (source + step) % count) for source in range(count)]


def swapped(part):
    return lax.ppermute(part, "c", ring(2, 1))


def hop_sum(blocks, axis):
    total = blocks[0].astype(f32)
    for step in (2, 1, 3):
        got = lax.ppermute(blocks[step].astype(bf16), axis, ring(4, step))
        total = total + got.astype(f32)
    return total


def further(total, position, axis):
    mine = lax.axis_index(axis)
    return [
        lax.dynamic_index_in_dim(total, (mine + step) % 4, position, keepdims=False)
        for step in range(4)
    ]


def sum_over_devices(own, got, out_own, out_got, policy):
    core = lax.axis_index("c")
    place = jnp.stack([lax.axis_index(axis) for axis in "xyz"])
    a_blocks, b_blocks, c_blocks = pair_sum(place, own, got, out_own, out_got, policy)
    a = hop_sum(a_blocks, "x")
    b = hop_sum(b_blocks, "y")
    c = hop_sum(c_blocks, "z")
    ac = [
        jnp.concatenate([left.astype(bf16), right.astype(bf16)], axis=2)
        for left, right in zip(further(a, 1, "y"), further(c, 0, "y"))
    ]
    ac = hop_sum(ac, "y")
    b = hop_sum(further(b, 1, "x"), "x")
    ab = jnp.concatenate([ac[:, :, :768], b], axis=2).astype(bf16).reshape(8, 8, 1536)
    ab = lax.all_to_all(ab, ("z", "c"), 0, 0, tiled=True).reshape(4, 2, 8, 1536)
    ab = jnp.sum(ab.astype(f32), axis=0)
    c = hop_sum(further(ac[:, :, 768:], 0, "x"), "x").reshape(2, 8, COLS_C)
    mine = lax.dynamic_index_in_dim(c, core, 0, keepdims=False)
    theirs = swapped(lax.dynamic_index_in_dim(c, 1 - core, 0, keepdims=False))
    c = jnp.stack([jnp.where(core == 0, mine, theirs), jnp.where(core == 0, theirs, mine)])
    out = jnp.concatenate([ab[:, :, 512:768], ab[:, :, 1280:]], axis=2)
    square = [ab[:, :, :512], ab[:, :, 768:1280], c[:, :, :HALF], out]
    columns = [part.transpose(1, 0, 2).reshape(8, WIDTH) for part in square]
    return jnp.concatenate([*columns, c[0, :, HALF:] + c[1, :, HALF:]], axis=1)


def body(
    states,
    norm_gain,
    w_query,
    w_keyval,
    w_out,
    rel_bias,
    w_policy,
    w_value,
    actions,
    legal_mask,
    rewards,
    episode_end,
    behavior_logprob,
    reg_logprob,
):
    core, segment = lax.axis_index("c"), lax.axis_index(TIME)
    states = states.reshape(ROWS, WIDTH)
    links = [(source, source + 1) for source in range(SEGS - 1)]
    mem_states = lax.ppermute(states, TIME, links)
    gain = norm_gain.reshape(1, WIDTH)
    steps = (legal_mask, actions, rewards, episode_end, behavior_logprob, reg_logprob)
    weights = (w_out, rel_bias, w_policy, w_value.reshape(1, WIDTH))

    qkv, turned = project(states, gain, w_query, w_keyval)
    has_memory = (segment > 0).astype(jnp.int32).reshape(1)
    mem_turned, kmem, vmem, probs, att_turned, hidden, stats, told = attend(
        has_memory, mem_states, gain, w_keyval, qkv, weights, states, steps
    )
    told = lax.all_to_all(told, TIME, 0, 0, tiled=True)
    att_cot, out_own, out_other, grad_policy = cotangents(
        segment.reshape(1), told, stats, steps, weights, hidden, att_turned
    )
    out_got = swapped(out_other)
    backward = functools.partial(
        heads_backward,
        att_cot=att_cot,
        probs=probs,
        qkv=qkv,
        kmem=kmem,
        vmem=vmem,
        turned=turned,
        mem_turned=mem_turned,
    )
    got = swapped(backward(first=(2 * (1 - core)).reshape(1)))
    owned = backward(first=(2 * core).reshape(1))
    raw_rows = sum_over_devices(owned, got, out_own, out_got, grad_policy)
    squares = jnp.sum(raw_rows * raw_rows)
    spread = jnp.broadcast_to(squares * (1.0 / 128.0), (128, 128))
    grand_total = jnp.sum(lax.all_to_all(spread, EVERY, 0, 0, tiled=True))
    entry_count = WIDTH * raw_rows.shape[1]
    clip_scale = jnp.minimum(1.0, math.sqrt(entry_count) / jnp.sqrt(grand_total + grad_eps))
    return raw_rows * clip_scale


def solution(mesh):
    fine = Mesh(mesh.devices.reshape(4, 4, 4, 2), EVERY)
    by_step = P("z", TIME)
    return jax.shard_map(
        body,
        mesh=fine,
        in_specs=(
            P("z", TIME, None),
            P(),
            P(),
            P(),
            P(),
            P(),
            P(),
            P(),
            by_step,
            P("z", TIME, None),
            by_step,
            by_step,
            by_step,
            by_step,
        ),
        out_specs=P(EVERY, None),
        check_vma=False,
    )
```
